512 devices in a mesh: row: 16 (over z), col: 32 (over y, x, core).
Axes of the slice: x: 4, y: 4, z: 16, core: 2. Of those that a mesh axis runs over, the one named last changes fastest.
Arguments:
- flow_state: bfloat16 [131072, 256], P(('col', 'row')), may hold values from -6 to 6
- link_state: bfloat16 [65536, 256], P(('row', 'col')), may hold values from -6 to 6
- incidence: bfloat16 [16, 32, 24, 128, 128], P('row', 'col'), may hold values from -0.29882812 to 0.29882812
- tile_flow: int32 [16, 32, 24], P('row', 'col'), may hold values from 0 to 31
- tile_link: int32 [16, 32, 24], P('row', 'col'), may hold values from 0 to 31
- tile_live: int32 [16, 32, 24], P('row', 'col'), may hold values from 0 to 1, as said below
- link_gain: float32 [256], replicated, may hold values from 0.5 to 2
- link_agg_weight: bfloat16 [256, 256], replicated, may hold values from -0.375 to 0.375
- link_self_weight: bfloat16 [256, 256], replicated, may hold values from -0.375 to 0.375
- link_out_weight: bfloat16 [256, 256], replicated, may hold values from -0.375 to 0.375
- flow_gain: float32 [256], replicated, may hold values from 0.5 to 2
- flow_agg_weight: bfloat16 [256, 256], replicated, may hold values from -0.375 to 0.375
- flow_self_weight: bfloat16 [256, 256], replicated, may hold values from -0.375 to 0.375
- flow_out_weight: bfloat16 [256, 256], replicated, may hold values from -0.375 to 0.375
Outputs:
- link_next: bfloat16 [65536, 256], P(('row', 'col'))
- flow_next: bfloat16 [131072, 256], P(('col', 'row'))
The draws below stay inside these ranges and needn't reach their ends.
Inputs may be any that keep to these rules, and one draw needn't show every extreme that they name: `tile_live`: in every draw some group pair has all 24 slots live; the number of live slots differs from pair to pair.
All inputs are finite; a program needn't handle non-finite values.
Results may differ from the reference program's by a relative error of at most 0.018.
Values may be sent and summed in bfloat16 or wider, within the bound.
No kernel may reach another device: no remote copies, remote signals or barrier semaphores. Data moves between devices by JAX's collectives and lax.ppermute only.
A program may use at most 64 MiB of HBM per device.

```python
import math
import jax
import jax.numpy as jnp
import numpy as np
from jax import lax

H = 256
BS = 128
TMAX = 24
LGROUPS = 16
FGROUPS = 32
FGB = 32
LGB = 32
FLOWS = 131072
LINKS = 65536


def draw_tile_live(key, part):
    key_level, key_pick, key_order = jax.random.split(jax.random.fold_in(key, 7), 3)
    pairs = LGROUPS * FGROUPS
    level = jax.random.randint(key_level, (pairs,), 1, 9)
    filled = jnp.maximum(TMAX * level * level // 64, 1)
    chosen = jax.random.randint(key_pick, (), 0, pairs)
    filled = jnp.where(jnp.arange(pairs) == chosen, TMAX, filled)
    scores = jax.random.randint(key_order, (pairs, TMAX), 0, 2 ** 20) * TMAX + jnp.arange(TMAX)[None, :]
    ranking = jnp.argsort(jnp.argsort(scores, axis=1), axis=1)
    living = (ranking < filled[:, None]).astype(jnp.int32)
    return living.reshape(LGROUPS, FGROUPS, TMAX)


def set_ends(drawn, rng, least, high):
    place = [jax.random.randint(jax.random.fold_in(rng, axis), (), 0, length) for axis, length in enumerate(drawn.shape)]
    widest = drawn.shape.index(max(drawn.shape))
    next_to = place[:widest] + [(place[widest] + 1) % drawn.shape[widest]] + place[widest + 1:]
    return drawn.at[tuple(place)].set(least).at[tuple(next_to)].set(high)


def block_levels(own_key, shape, cuts, least, largest):
    loudness, own = 1.0, jax.random.fold_in(own_key, 6)
    for position, blocks in cuts:
        draws = jnp.exp(jax.random.uniform(jax.random.fold_in(own, position), (blocks,), jnp.float32, least / len(cuts), largest / len(cuts)))
        loudness = loudness * jnp.repeat(draws, shape[position] // blocks).reshape([-1 if axis == position else 1 for axis in range(len(shape))])
    return loudness


def rank_table(amount, slope):
    loads = [(1 << 20) // math.isqrt(rank ** slope) + 1 for rank in range(1, amount + 1)]
    width = 1 + sum(loads) // (1 << 30)
    return np.cumsum(np.array([max(1, weight // width) for weight in loads]))


def skewed_ids(rng, shape, count, lean):
    table = rank_table(count, lean)
    lot = jax.random.randint(jax.random.fold_in(rng, 1), shape, 0, int(table[count - 1]))
    rank = jnp.searchsorted(jnp.asarray(table, jnp.int32), lot, side="right")
    return jax.random.permutation(jax.random.fold_in(rng, 2), count)[rank].astype(jnp.int32)


def scatter_about(stream_key, shape, width, limit, cuts=(), held_as=jnp.bfloat16):
    array = width * jax.random.normal(stream_key, shape, jnp.float32)
    if cuts:
        array = array * block_levels(stream_key, shape, cuts, -0.22, 0.18)
    return jnp.clip(array, -limit, limit).astype(held_as)


def setup_inputs(seed: int = 0) -> dict:
    splits = jax.random.split(jax.random.key(seed), 15)
    flow_state = scatter_about(splits[0], (FLOWS, H), 1.0, 6.0, ((0, 512),))
    link_state = scatter_about(splits[1], (LINKS, H), 1.0, 6.0, ((0, 512),))
    incidence = scatter_about(splits[2], (LGROUPS, FGROUPS, TMAX, BS, BS), 0.05, 0.29882812, ((0, 16), (1, 32)))
    tile_flow = set_ends(jax.random.randint(splits[3], (LGROUPS, FGROUPS, TMAX), 0, FGB), jax.random.fold_in(splits[3], 1), 0, FGB - 1).astype(jnp.int32)
    tile_link = set_ends(skewed_ids(splits[4], (LGROUPS, FGROUPS, TMAX), LGB, 2), jax.random.fold_in(splits[4], 3), 0, LGB - 1).astype(jnp.int32)
    tile_live = draw_tile_live(jax.random.fold_in(splits[14], 71), 0)
    link_gain = jnp.clip(jnp.exp(jax.random.uniform(splits[6], (H,), jnp.float32, math.log(0.5), math.log(2.0))), 0.5, 2.0)
    link_agg_weight = scatter_about(splits[7], (H, H), H ** -0.5, 0.375)
    link_self_weight = scatter_about(splits[8], (H, H), H ** -0.5, 0.375)
    link_out_weight = scatter_about(splits[9], (H, H), H ** -0.5, 0.375)
    flow_gain = jnp.clip(jnp.exp(jax.random.uniform(splits[10], (H,), jnp.float32, math.log(0.5), math.log(2.0))), 0.5, 2.0)
    flow_agg_weight = scatter_about(splits[11], (H, H), H ** -0.5, 0.375)
    flow_self_weight = scatter_about(splits[12], (H, H), H ** -0.5, 0.375)
    flow_out_weight = scatter_about(splits[13], (H, H), H ** -0.5, 0.375)
    return dict(flow_state=flow_state, link_state=link_state, incidence=incidence, tile_flow=tile_flow, tile_link=tile_link, tile_live=tile_live, link_gain=link_gain, link_agg_weight=link_agg_weight, link_self_weight=link_self_weight, link_out_weight=link_out_weight, flow_gain=flow_gain, flow_agg_weight=flow_agg_weight, flow_self_weight=flow_self_weight, flow_out_weight=flow_out_weight)


def state_update(totals, state, gain, agg_weight, self_weight, out_weight):
    scale = lax.rsqrt(lax.optimization_barrier(jnp.mean(totals * totals, axis=-1, keepdims=True)) + 1e-05)
    normed = (totals * scale * gain).astype(jnp.bfloat16)
    before = jnp.dot(normed, agg_weight, preferred_element_type=jnp.float32) + jnp.dot(state, self_weight, preferred_element_type=jnp.float32)
    hidden = jax.nn.silu(before).astype(jnp.bfloat16)
    return (state.astype(jnp.float32) + jnp.dot(hidden, out_weight, preferred_element_type=jnp.float32)).astype(jnp.bfloat16)

def block_sums(coefs, pieces, targets, live_slots, block_count, to_links):
    if to_links:
        products = jnp.einsum('tij,tih->tjh', coefs.astype(jnp.float32), pieces.astype(jnp.float32))
    else:
        products = jnp.einsum('tij,tjh->tih', coefs.astype(jnp.float32), pieces.astype(jnp.float32))
    select = (targets[None, :] == jnp.arange(block_count, dtype=jnp.int32)[:, None]).astype(jnp.float32)
    select = select * live_slots.astype(jnp.float32)[None, :]
    return jnp.dot(select, products.reshape(products.shape[0], -1), precision=lax.Precision.HIGHEST)

def rounded(term):
    return lax.optimization_barrier(term.astype(jnp.bfloat16)).astype(jnp.float32)

def reference(flow_state, link_state, incidence, tile_flow, tile_link, tile_live, link_gain, link_agg_weight, link_self_weight, link_out_weight, flow_gain, flow_agg_weight, flow_self_weight, flow_out_weight):
    flow_groups = flow_state.reshape(FGROUPS, FGB, BS, H)

    def link_group_sum(link_index):

        def add_group(total, flow_index):
            pieces = jnp.take(flow_groups[flow_index], tile_flow[link_index, flow_index], axis=0)
            term = block_sums(incidence[link_index, flow_index], pieces, tile_link[link_index, flow_index], tile_live[link_index, flow_index], LGB, True)
            return (total + rounded(term), None)
        total, _ = lax.scan(add_group, jnp.zeros((LGB, BS * H), jnp.float32), jnp.arange(FGROUPS, dtype=jnp.int32))
        return total
    link_sum = lax.map(link_group_sum, jnp.arange(LGROUPS, dtype=jnp.int32)).reshape(LINKS, H)
    link_next = state_update(link_sum, link_state, link_gain, link_agg_weight, link_self_weight, link_out_weight)
    link_groups = link_next.reshape(LGROUPS, LGB, BS, H)

    def flow_group_sum(flow_index):

        def add_group(total, link_index):
            pieces = jnp.take(link_groups[link_index], tile_link[link_index, flow_index], axis=0)
            term = block_sums(incidence[link_index, flow_index], pieces, tile_flow[link_index, flow_index], tile_live[link_index, flow_index], FGB, False)
            return (total + rounded(term), None)
        total, _ = lax.scan(add_group, jnp.zeros((FGB, BS * H), jnp.float32), jnp.arange(LGROUPS, dtype=jnp.int32))
        return total
    flow_sum = lax.map(flow_group_sum, jnp.arange(FGROUPS, dtype=jnp.int32)).reshape(FLOWS, H)
    flow_next = state_update(flow_sum, flow_state, flow_gain, flow_agg_weight, flow_self_weight, flow_out_weight)
    return (link_next, flow_next)
```

```python
import functools
import jax
import jax.numpy as jnp
from jax import lax
from jax.experimental import pallas as pl
from jax.experimental.pallas import tpu as pltpu
from jax.sharding import PartitionSpec as P

H = 256
BS = 128
VMEM = pl.BlockSpec(memory_space=pltpu.VMEM)
SMEM = pl.BlockSpec(memory_space=pltpu.SMEM)


def products_kernel(to_links, take_ref, put_ref, live_ref, coefs_ref, pieces_ref, out_ref, acc_ref):
    blocks = out_ref.shape[0]
    acc_ref[...] = jnp.zeros_like(acc_ref)
    for slot in range(coefs_ref.shape[0]):
        put = jnp.where(live_ref[0, 0, slot] == 1, put_ref[0, 0, slot], blocks)
        term = lax.dot_general(
            coefs_ref[slot],
            pieces_ref[take_ref[0, 0, slot]],
            (((0 if to_links else 1,), (0,)), ((), ())),
            preferred_element_type=jnp.float32,
        )
        acc_ref[put] += term
    out_ref[...] = acc_ref[:blocks].astype(out_ref.dtype)


def products(to_links, take, put, live, coefs, pieces, blocks):
    width = pieces.shape[-1]
    return pl.pallas_call(
        functools.partial(products_kernel, to_links),
        out_shape=jax.ShapeDtypeStruct((blocks, BS, width), jnp.bfloat16),
        in_specs=[SMEM, SMEM, SMEM, VMEM, VMEM],
        out_specs=VMEM,
        scratch_shapes=[pltpu.VMEM((blocks + 1, BS, width), jnp.float32)],
        compiler_params=pltpu.CompilerParams(vmem_limit_bytes=32 << 20),
        name="link_products" if to_links else "flow_products",
    )(take, put, live, coefs, pieces)


def update_kernel(parts_ref, state_ref, gain_ref, agg_ref, self_ref, out_w_ref, *out_refs):
    totals = jnp.sum(parts_ref[...].astype(jnp.float32), axis=0)
    scale = lax.rsqrt(jnp.mean(totals * totals, axis=-1, keepdims=True) + 1e-05)
    normed = (totals * scale * gain_ref[...]).astype(jnp.bfloat16)
    before = jnp.dot(normed, agg_ref[...], preferred_element_type=jnp.float32) + jnp.dot(
        state_ref[...], self_ref[...], preferred_element_type=jnp.float32
    )
    hidden = jax.nn.silu(before).astype(jnp.bfloat16)
    result = (
        state_ref[...].astype(jnp.float32)
        + jnp.dot(hidden, out_w_ref[...], preferred_element_type=jnp.float32)
    ).astype(jnp.bfloat16)
    out_refs[0][...] = result
    if len(out_refs) > 1:
        for copy in range(out_refs[1].shape[0]):
            out_refs[1][copy] = result


def update(parts, state, gain, agg_weight, self_weight, out_weight, copies):
    shapes = [jax.ShapeDtypeStruct(state.shape, jnp.bfloat16)]
    if copies:
        shapes.append(jax.ShapeDtypeStruct((copies,) + state.shape, jnp.bfloat16))
    return pl.pallas_call(
        update_kernel,
        out_shape=shapes,
        in_specs=[VMEM] * 6,
        out_specs=[VMEM] * len(shapes),
        compiler_params=pltpu.CompilerParams(vmem_limit_bytes=32 << 20),
        name="link_update" if copies else "flow_update",
    )(parts, state, gain.reshape(1, H), agg_weight, self_weight, out_weight)


def on_device(
    flow_state,
    link_state,
    incidence,
    tile_flow,
    tile_link,
    tile_live,
    link_gain,
    link_agg_weight,
    link_self_weight,
    link_out_weight,
    flow_gain,
    flow_agg_weight,
    flow_self_weight,
    flow_out_weight,
):
    coefs = incidence[0, 0]
    cols = lax.axis_size("col")
    rows = lax.axis_size("row")
    flow_group = lax.all_gather(flow_state, "row", axis=0, tiled=True)
    flow_blocks = flow_state.shape[0] // BS * rows
    link_blocks = link_state.shape[0] // BS * cols
    link_part = products(
        True, tile_flow, tile_link, tile_live, coefs,
        flow_group.reshape(flow_blocks, BS, H), link_blocks,
    )
    link_parts = lax.all_to_all(link_part, "col", 0, 0, tiled=True)
    link_next, link_copies = update(
        link_parts, link_state, link_gain, link_agg_weight, link_self_weight, link_out_weight, cols
    )
    link_group = lax.all_to_all(link_copies, "col", 0, 0, tiled=True)
    flow_part = products(
        False, tile_link, tile_flow, tile_live, coefs, link_group, flow_blocks
    )
    flow_sum = lax.psum_scatter(
        flow_part.reshape(flow_blocks * BS, H), "row", scatter_dimension=0, tiled=True
    )
    (flow_next,) = update(
        flow_sum[None], flow_state, flow_gain, flow_agg_weight, flow_self_weight, flow_out_weight, 0
    )
    return (link_next, flow_next)


def solution(mesh):
    return jax.shard_map(
        on_device,
        mesh=mesh,
        in_specs=(
            P(("col", "row"), None),
            P(("row", "col"), None),
            P("row", "col", None, None, None),
            P("row", "col", None),
            P("row", "col", None),
            P("row", "col", None),
            P(),
            P(),
            P(),
            P(),
            P(),
            P(),
            P(),
            P(),
        ),
        out_specs=(P(("row", "col"), None), P(("col", "row"), None)),
        check_vma=False,
    )
```

```python
import functools
import jax
import jax.numpy as jnp
from jax import lax
from jax.experimental import pallas as pl
from jax.experimental.pallas import tpu as pltpu
from jax.sharding import PartitionSpec as P

H = 256
BS = 128
VMEM = pl.BlockSpec(memory_space=pltpu.VMEM)
SMEM = pl.BlockSpec(memory_space=pltpu.SMEM)
PARAMS = pltpu.CompilerParams(vmem_limit_bytes=40 << 20)
F32 = jnp.float32
BF16 = jnp.bfloat16
SCALE = 8192.0


def link_products_kernel(
    me_ref, flow_ref, link_ref, live_ref, coefs_ref, pieces_ref, own_ref, other_ref, acc_ref
):
    blocks = acc_ref.shape[0] - 1
    half = blocks // 2
    acc_ref[...] = jnp.zeros_like(acc_ref)
    for slot in range(coefs_ref.shape[0]):
        block = link_ref[0, 0, slot]
        place = ((block + me_ref[1]) % 2) * half + block // 2
        place = jnp.where(live_ref[0, 0, slot] == 1, place, blocks)
        acc_ref[place] += lax.dot_general(
            coefs_ref[slot],
            pieces_ref[flow_ref[0, 0, slot]],
            (((0,), (0,)), ((), ())),
            preferred_element_type=F32,
        )
    own_ref[...] = acc_ref[:half].astype(BF16)
    other_ref[...] = acc_ref[half : 2 * half].astype(BF16)


def link_products(me, flow, link, live, coefs, pieces, blocks):
    shape = jax.ShapeDtypeStruct((blocks // 2, BS, H), BF16)
    return pl.pallas_call(
        link_products_kernel,
        out_shape=[shape, shape],
        in_specs=[SMEM, SMEM, SMEM, SMEM, VMEM, VMEM],
        out_specs=[VMEM, VMEM],
        scratch_shapes=[pltpu.VMEM((blocks + 1, BS, H), F32)],
        compiler_params=PARAMS,
        name="link_products",
    )(me, flow, link, live, coefs, pieces)


def flow_products_kernel(
    me_ref, flow_ref, link_ref, live_ref, coefs_ref, own_ref, other_ref,
    same_ref, next_ref, far_up_ref, far_down_ref, prev_ref, acc_ref, pieces_ref,
):
    blocks = acc_ref.shape[0] - 1
    quarter = blocks // 4
    half = own_ref.shape[0]
    pieces_ref[:half] = own_ref[...]
    pieces_ref[half:] = other_ref[...]
    acc_ref[...] = jnp.zeros_like(acc_ref)
    for slot in range(coefs_ref.shape[0]):
        block = flow_ref[0, 0, slot]
        row = block // 2
        place = ((row - me_ref[0] + 16) % 4) * quarter + (row // 4) * 2 + block % 2
        place = jnp.where(live_ref[0, 0, slot] == 1, place, blocks)
        piece = link_ref[0, 0, slot]
        piece = ((piece + me_ref[1]) % 2) * half + piece // 2
        acc_ref[place] += jnp.dot(
            coefs_ref[slot], pieces_ref[piece], preferred_element_type=F32
        )
    low = quarter // 2
    same_ref[...] = acc_ref[:quarter].astype(BF16)
    next_ref[...] = acc_ref[quarter : 2 * quarter].astype(BF16)
    far_up_ref[...] = acc_ref[2 * quarter : 2 * quarter + low].astype(BF16)
    far_down_ref[...] = acc_ref[2 * quarter + low : 3 * quarter].astype(BF16)
    prev_ref[...] = acc_ref[3 * quarter : 4 * quarter].astype(BF16)


def flow_products(me, flow, link, live, coefs, own, other, blocks):
    whole = jax.ShapeDtypeStruct((blocks // 4, BS, H), BF16)
    part = jax.ShapeDtypeStruct((blocks // 8, BS, H), BF16)
    return pl.pallas_call(
        flow_products_kernel,
        out_shape=[whole, whole, part, part, whole],
        in_specs=[SMEM, SMEM, SMEM, SMEM, VMEM, VMEM, VMEM],
        out_specs=[VMEM] * 5,
        scratch_shapes=[
            pltpu.VMEM((blocks + 1, BS, H), F32),
            pltpu.VMEM((2 * own.shape[0], BS, H), BF16),
        ],
        compiler_params=PARAMS,
        name="flow_products",
    )(me, flow, link, live, coefs, own, other)


def add_kernel(a_ref, b_ref, out_ref):
    out_ref[...] = (a_ref[...].astype(F32) + b_ref[...].astype(F32)).astype(BF16)


def add_two(a, b):
    return pl.pallas_call(
        add_kernel,
        out_shape=jax.ShapeDtypeStruct(a.shape, BF16),
        in_specs=[VMEM, VMEM],
        out_specs=VMEM,
        compiler_params=PARAMS,
        name="add_two",
    )(a, b)


def relay_kernel(up_ref, low_ref, down_ref, high_ref, up_out_ref, down_out_ref):
    half = low_ref.shape[0]
    up_out_ref[:half] = (up_ref[:half].astype(F32) + low_ref[...].astype(F32)).astype(BF16)
    up_out_ref[half:] = up_ref[half:]
    down_out_ref[:half] = down_ref[:half]
    down_out_ref[half:] = (down_ref[half:].astype(F32) + high_ref[...].astype(F32)).astype(BF16)


def relay(up, low, down, high):
    return pl.pallas_call(
        relay_kernel,
        out_shape=[jax.ShapeDtypeStruct(up.shape, BF16)] * 2,
        in_specs=[VMEM] * 4,
        out_specs=[VMEM] * 2,
        compiler_params=PARAMS,
        name="relay",
    )(up, low, down, high)


def add_three_kernel(a_ref, b_ref, c_ref, out_ref):
    out_ref[...] = (
        a_ref[...].astype(F32) + b_ref[...].astype(F32) + c_ref[...].astype(F32)
    ).astype(BF16)


def add_three(a, b, c):
    return pl.pallas_call(
        add_three_kernel,
        out_shape=jax.ShapeDtypeStruct(a.shape, BF16),
        in_specs=[VMEM] * 3,
        out_specs=VMEM,
        compiler_params=PARAMS,
        name="add_three",
    )(a, b, c)


def update_kernel(parts_ref, state_ref, gain_ref, agg_ref, self_ref, out_w_ref, *out_refs):
    totals = jnp.sum(parts_ref[...].astype(F32), axis=0)
    scale = lax.rsqrt(jnp.mean(totals * totals, axis=-1, keepdims=True) + 1e-05)
    normed = (totals * scale * gain_ref[...]).astype(BF16)
    before = jnp.dot(normed, agg_ref[...], preferred_element_type=F32) + jnp.dot(
        state_ref[...], self_ref[...], preferred_element_type=F32
    )
    hidden = jax.nn.silu(before).astype(BF16)
    result = (
        state_ref[...].astype(F32)
        + jnp.dot(hidden, out_w_ref[...], preferred_element_type=F32)
    ).astype(BF16)
    out_refs[0][...] = result
    if len(out_refs) > 1:
        for copy in range(out_refs[1].shape[0]):
            out_refs[1][copy] = result


def update(parts, state, gain, agg_weight, self_weight, out_weight, copies):
    shapes = [jax.ShapeDtypeStruct(state.shape, BF16)]
    if copies:
        shapes.append(jax.ShapeDtypeStruct((copies,) + state.shape, BF16))
    return pl.pallas_call(
        update_kernel,
        out_shape=shapes,
        in_specs=[VMEM] * 6,
        out_specs=[VMEM] * len(shapes),
        compiler_params=PARAMS,
        name="link_update" if copies else "flow_update",
    )(parts, state, gain.reshape(1, H), agg_weight, self_weight, out_weight)


def on_device(
    flow_state,
    link_state,
    incidence,
    tile_flow,
    tile_link,
    tile_live,
    link_gain,
    link_agg_weight,
    link_self_weight,
    link_out_weight,
    flow_gain,
    flow_agg_weight,
    flow_self_weight,
    flow_out_weight,
):
    coefs = incidence[0, 0]
    cols = lax.axis_size("col")
    rows = lax.axis_size("row")
    pairs = cols // 2
    flow_blocks = flow_state.shape[0] // BS * rows
    me = jnp.stack([lax.axis_index("row"), lax.axis_index("col") % 2]).astype(jnp.int32)
    sibling = [(i, i ^ 1) for i in range(cols)]
    same_core = [[2 * i + core for i in range(pairs)] for core in range(2)]
    up = [(i, (i + 1) % rows) for i in range(rows)]
    down = [(i, (i - 1) % rows) for i in range(rows)]
    far = [[4 * a + b for a in range(rows // 4)] for b in range(4)]

    flow_group = gather_rows(flow_state)
    own, other = link_products(
        me, tile_flow, tile_link, tile_live, coefs,
        flow_group.reshape(flow_blocks, BS, H), cols,
    )
    own = add_two(own, lax.ppermute(other, "col", sibling))
    link_parts = lax.all_to_all(own, "col", 0, 0, tiled=True, axis_index_groups=same_core)
    link_next, link_copies = update(
        link_parts, link_state, link_gain, link_agg_weight, link_self_weight, link_out_weight, pairs
    )
    own = lax.all_to_all(link_copies, "col", 0, 0, tiled=True, axis_index_groups=same_core)
    other = lax.ppermute(own, "col", sibling)
    same, nxt, low, high, prev = flow_products(
        me, tile_flow, tile_link, tile_live, coefs, own, other, flow_blocks
    )
    low = lax.ppermute(low, "row", up)
    high = lax.ppermute(high, "row", down)
    nxt, prev = relay(nxt, low, prev, high)
    nxt = lax.ppermute(nxt, "row", up)
    prev = lax.ppermute(prev, "row", down)
    same = add_three(same, nxt, prev)
    per = flow_state.shape[0]
    flow_parts = lax.all_to_all(
        same.reshape(rows // 4, per, H), "row", 0, 0, tiled=True, axis_index_groups=far
    )
    (flow_next,) = update(
        flow_parts, flow_state, flow_gain, flow_agg_weight, flow_self_weight, flow_out_weight, 0
    )
    return (link_next, flow_next)


def gather_rows(state):
    sent = (state.astype(F32) * SCALE).astype(jnp.float16)
    got = lax.all_gather(sent, "row", axis=0, tiled=True)
    return (got.astype(F32) * (1 / SCALE)).astype(BF16)


def solution(mesh):
    return jax.shard_map(
        on_device,
        mesh=mesh,
        in_specs=(
            P(("col", "row"), None),
            P(("row", "col"), None),
            P("row", "col", None, None, None),
            P("row", "col", None),
            P("row", "col", None),
            P("row", "col", None),
            P(),
            P(),
            P(),
            P(),
            P(),
            P(),
            P(),
            P(),
        ),
        out_specs=(P(("row", "col"), None), P(("col", "row"), None)),
        check_vma=False,
    )
```

```python
import functools
import jax
import jax.numpy as jnp
from jax import lax
from jax.experimental import pallas as pl
from jax.experimental.pallas import tpu as pltpu
from jax.sharding import PartitionSpec as P

H = 256
BS = 128
VMEM = pl.BlockSpec(memory_space=pltpu.VMEM)
SMEM = pl.BlockSpec(memory_space=pltpu.SMEM)
PARAMS = pltpu.CompilerParams(vmem_limit_bytes=40 << 20)
F32 = jnp.float32
BF16 = jnp.bfloat16
SCALE = 8192.0


def link_products_kernel(
    me_ref, flow_ref, link_ref, live_ref, coefs_ref, pieces_ref, own_ref, other_ref, acc_ref
):
    blocks = acc_ref.shape[0] - 1
    half = blocks // 2
    acc_ref[...] = jnp.zeros_like(acc_ref)
    for slot in range(coefs_ref.shape[0]):
        block = link_ref[0, 0, slot]
        place = ((block + me_ref[1]) % 2) * half + block // 2
        place = jnp.where(live_ref[0, 0, slot] == 1, place, blocks)
        acc_ref[place] += lax.dot_general(
            coefs_ref[slot],
            pieces_ref[flow_ref[0, 0, slot]],
            (((0,), (0,)), ((), ())),
            preferred_element_type=F32,
        )
    own_ref[...] = acc_ref[:half].astype(BF16)
    other_ref[...] = acc_ref[half : 2 * half].astype(BF16)


def link_products(me, flow, link, live, coefs, pieces, blocks):
    shape = jax.ShapeDtypeStruct((blocks // 2, BS, H), BF16)
    return pl.pallas_call(
        link_products_kernel,
        out_shape=[shape, shape],
        in_specs=[SMEM, SMEM, SMEM, SMEM, VMEM, VMEM],
        out_specs=[VMEM, VMEM],
        scratch_shapes=[pltpu.VMEM((blocks + 1, BS, H), F32)],
        compiler_params=PARAMS,
        name="link_products",
    )(me, flow, link, live, coefs, pieces)


def flow_products_kernel(
    me_ref, flow_ref, link_ref, live_ref, coefs_ref, own_ref, other_ref, *rest
):
    *out_refs, acc_ref, pieces_ref = rest
    blocks = acc_ref.shape[0] - 1
    rows = blocks // 2
    half = own_ref.shape[0]
    pieces_ref[:half] = own_ref[...]
    pieces_ref[half:] = other_ref[...]
    acc_ref[...] = jnp.zeros_like(acc_ref)
    for slot in range(coefs_ref.shape[0]):
        block = flow_ref[0, 0, slot]
        ahead = (block // 2 - me_ref[0] + rows) % rows
        upward = ahead < rows // 2
        steps = jnp.where(upward, ahead, (rows - ahead) % (rows // 2))
        odd = me_ref[0] % 2
        second = jnp.where(steps == 0, jnp.where(ahead == 0, 0, 1), jnp.where(upward, odd, 1 - odd))
        place = second * rows + steps * 2 + block % 2
        place = jnp.where(live_ref[0, 0, slot] == 1, place, blocks)
        piece = link_ref[0, 0, slot]
        piece = ((piece + me_ref[1]) % 2) * half + piece // 2
        acc_ref[place] += jnp.dot(
            coefs_ref[slot], pieces_ref[piece], preferred_element_type=F32
        )
    start = 0
    for out_ref in out_refs:
        count = out_ref.shape[0]
        out_ref[...] = acc_ref[start : start + count].astype(BF16)
        start += count


def flow_products(me, flow, link, live, coefs, own, other, blocks):
    row = jax.ShapeDtypeStruct((2, BS, H), BF16)
    half_row = jax.ShapeDtypeStruct((1, BS, H), BF16)
    shapes = [row] * (blocks // 4) + [half_row] * 2 + [row] * (blocks // 4 - 1)
    outs = pl.pallas_call(
        flow_products_kernel,
        out_shape=shapes,
        in_specs=[SMEM, SMEM, SMEM, SMEM, VMEM, VMEM, VMEM],
        out_specs=[VMEM] * len(shapes),
        scratch_shapes=[
            pltpu.VMEM((blocks + 1, BS, H), F32),
            pltpu.VMEM((2 * own.shape[0], BS, H), BF16),
        ],
        compiler_params=PARAMS,
        name="flow_products",
    )(me, flow, link, live, coefs, own, other)
    side = blocks // 4
    return outs[0], outs[1:side], outs[side], outs[side + 1], outs[side + 2 :]


def add(a, b):
    return (a.astype(F32) + b.astype(F32)).astype(BF16)


def sum_over_rows(mine, for_a, half_a, half_b, for_b, rows):
    swap_a = [(i, i ^ 1) for i in range(rows)]
    swap_b = [(i, ((i - 1) ^ 1) + 1 if i % rows else rows - 1) for i in range(rows)]
    swap_b = [(i, j % rows) for i, j in swap_b]
    got_a = lax.ppermute(half_a, "row", swap_a)
    got_b = lax.ppermute(half_b, "row", swap_b)
    a = jnp.concatenate([for_a[-1][:1], add(for_a[-1][1:], got_b)], axis=0)
    b = jnp.concatenate([add(for_b[-1][:1], got_a), for_b[-1][1:]], axis=0)
    for step in range(len(for_a) - 2, -2, -1):
        got_a = lax.ppermute(a, "row", swap_a)
        got_b = lax.ppermute(b, "row", swap_b)
        if step >= 0:
            b = add(for_b[step], got_a)
            a = add(for_a[step], got_b)
    return jnp.stack([x.reshape(2 * BS, H) for x in (mine, got_a, got_b)])


def add_kernel(a_ref, b_ref, out_ref):
    out_ref[...] = (a_ref[...].astype(F32) + b_ref[...].astype(F32)).astype(BF16)


def add_two(a, b):
    return pl.pallas_call(
        add_kernel,
        out_shape=jax.ShapeDtypeStruct(a.shape, BF16),
        in_specs=[VMEM, VMEM],
        out_specs=VMEM,
        compiler_params=PARAMS,
        name="add_two",
    )(a, b)


def update_kernel(parts_ref, state_ref, gain_ref, agg_ref, self_ref, out_w_ref, *out_refs):
    totals = jnp.sum(parts_ref[...].astype(F32), axis=0)
    scale = lax.rsqrt(jnp.mean(totals * totals, axis=-1, keepdims=True) + 1e-05)
    normed = (totals * scale * gain_ref[...]).astype(BF16)
    before = jnp.dot(normed, agg_ref[...], preferred_element_type=F32) + jnp.dot(
        state_ref[...], self_ref[...], preferred_element_type=F32
    )
    hidden = jax.nn.silu(before).astype(BF16)
    result = (
        state_ref[...].astype(F32)
        + jnp.dot(hidden, out_w_ref[...], preferred_element_type=F32)
    ).astype(BF16)
    out_refs[0][...] = result
    if len(out_refs) > 1:
        for copy in range(out_refs[1].shape[0]):
            out_refs[1][copy] = result


def update(parts, state, gain, agg_weight, self_weight, out_weight, copies):
    shapes = [jax.ShapeDtypeStruct(state.shape, BF16)]
    if copies:
        shapes.append(jax.ShapeDtypeStruct((copies,) + state.shape, BF16))
    return pl.pallas_call(
        update_kernel,
        out_shape=shapes,
        in_specs=[VMEM] * 6,
        out_specs=[VMEM] * len(shapes),
        compiler_params=PARAMS,
        name="link_update" if copies else "flow_update",
    )(parts, state, gain.reshape(1, H), agg_weight, self_weight, out_weight)


def on_device(
    flow_state,
    link_state,
    incidence,
    tile_flow,
    tile_link,
    tile_live,
    link_gain,
    link_agg_weight,
    link_self_weight,
    link_out_weight,
    flow_gain,
    flow_agg_weight,
    flow_self_weight,
    flow_out_weight,
):
    coefs = incidence[0, 0]
    cols = lax.axis_size("col")
    rows = lax.axis_size("row")
    pairs = cols // 2
    flow_blocks = flow_state.shape[0] // BS * rows
    me = jnp.stack([lax.axis_index("row"), lax.axis_index("col") % 2]).astype(jnp.int32)
    sibling = [(i, i ^ 1) for i in range(cols)]
    same_core = [[2 * i + core for i in range(pairs)] for core in range(2)]

    flow_group = gather_rows(flow_state)
    own, other = link_products(
        me, tile_flow, tile_link, tile_live, coefs,
        flow_group.reshape(flow_blocks, BS, H), cols,
    )
    own = add_two(own, lax.ppermute(other, "col", sibling))
    link_parts = lax.all_to_all(own, "col", 0, 0, tiled=True, axis_index_groups=same_core)
    link_next, link_copies = update(
        link_parts, link_state, link_gain, link_agg_weight, link_self_weight, link_out_weight, pairs
    )
    own = lax.all_to_all(link_copies, "col", 0, 0, tiled=True, axis_index_groups=same_core)
    other = lax.ppermute(own, "col", sibling)
    mine, for_a, half_a, half_b, for_b = flow_products(
        me, tile_flow, tile_link, tile_live, coefs, own, other, flow_blocks
    )
    flow_parts = sum_over_rows(mine, for_a, half_a, half_b, for_b, rows)
    (flow_next,) = update(
        flow_parts, flow_state, flow_gain, flow_agg_weight, flow_self_weight, flow_out_weight, 0
    )
    return (link_next, flow_next)


def gather_rows(state):
    sent = (state.astype(F32) * SCALE).astype(jnp.float16)
    got = lax.all_gather(sent, "row", axis=0, tiled=True)
    return (got.astype(F32) * (1 / SCALE)).astype(BF16)


def solution(mesh):
    return jax.shard_map(
        on_device,
        mesh=mesh,
        in_specs=(
            P(("col", "row"), None),
            P(("row", "col"), None),
            P("row", "col", None, None, None),
            P("row", "col", None),
            P("row", "col", None),
            P("row", "col", None),
            P(),
            P(),
            P(),
            P(),
            P(),
            P(),
            P(),
            P(),
        ),
        out_specs=(P(("row", "col"), None), P(("col", "row"), None)),
        check_vma=False,
    )
```

```python
import functools
import jax
import jax.numpy as jnp
from jax import lax
from jax.experimental import pallas as pl
from jax.experimental.pallas import tpu as pltpu
from jax.sharding import PartitionSpec as P

H = 256
BS = 128
VMEM = pl.BlockSpec(memory_space=pltpu.VMEM)
SMEM = pl.BlockSpec(memory_space=pltpu.SMEM)
PARAMS = pltpu.CompilerParams(vmem_limit_bytes=40 << 20)
F32 = jnp.float32
BF16 = jnp.bfloat16
SCALE = 8192.0


def link_products_kernel(
    me_ref, flow_ref, link_ref, live_ref, coefs_ref, pieces_ref, own_ref, other_ref, acc_ref
):
    blocks = acc_ref.shape[0] - 1
    half = blocks // 2
    acc_ref[...] = jnp.zeros_like(acc_ref)
    for slot in range(coefs_ref.shape[0]):
        block = link_ref[0, 0, slot]
        place = ((block + me_ref[1]) % 2) * half + block // 2
        place = jnp.where(live_ref[0, 0, slot] == 1, place, blocks)
        acc_ref[place] += lax.dot_general(
            coefs_ref[slot],
            pieces_ref[flow_ref[0, 0, slot]],
            (((0,), (0,)), ((), ())),
            preferred_element_type=F32,
        )
    own_ref[...] = acc_ref[:half].astype(BF16)
    other_ref[...] = acc_ref[half : 2 * half].astype(BF16)


def link_products(me, flow, link, live, coefs, pieces, blocks):
    shape = jax.ShapeDtypeStruct((blocks // 2, BS, H), BF16)
    return pl.pallas_call(
        link_products_kernel,
        out_shape=[shape, shape],
        in_specs=[SMEM, SMEM, SMEM, SMEM, VMEM, VMEM],
        out_specs=[VMEM, VMEM],
        scratch_shapes=[pltpu.VMEM((blocks + 1, BS, H), F32)],
        compiler_params=PARAMS,
        name="link_products",
    )(me, flow, link, live, coefs, pieces)


def flow_products_kernel(
    me_ref, flow_ref, link_ref, live_ref, coefs_ref, own_ref, other_ref, *rest
):
    *out_refs, acc_ref, pieces_ref = rest
    blocks = acc_ref.shape[0] - 1
    quarter = blocks // 4
    half = own_ref.shape[0]
    pieces_ref[:half] = own_ref[...]
    pieces_ref[half:] = other_ref[...]
    acc_ref[...] = jnp.zeros_like(acc_ref)
    for slot in range(coefs_ref.shape[0]):
        block = flow_ref[0, 0, slot]
        row = block // 2
        ahead = jnp.where(me_ref[0] % 2 == 0, row - me_ref[0], me_ref[0] - row)
        place = ((ahead + 2 * blocks) % 4) * quarter + (row // 4) * 2 + block % 2
        place = jnp.where(live_ref[0, 0, slot] == 1, place, blocks)
        piece = link_ref[0, 0, slot]
        piece = ((piece + me_ref[1]) % 2) * half + piece // 2
        acc_ref[place] += jnp.dot(
            coefs_ref[slot], pieces_ref[piece], preferred_element_type=F32
        )
    start = 0
    for out_ref in out_refs:
        count = out_ref.shape[0]
        out_ref[...] = acc_ref[start : start + count].astype(BF16)
        start += count


def flow_products(me, flow, link, live, coefs, own, other, blocks):
    counts = [blocks // 4, blocks // 4, blocks // 8, blocks // 8, blocks // 4]
    return pl.pallas_call(
        flow_products_kernel,
        out_shape=[jax.ShapeDtypeStruct((count, BS, H), BF16) for count in counts],
        in_specs=[SMEM, SMEM, SMEM, SMEM, VMEM, VMEM, VMEM],
        out_specs=[VMEM] * len(counts),
        scratch_shapes=[
            pltpu.VMEM((blocks + 1, BS, H), F32),
            pltpu.VMEM((2 * own.shape[0], BS, H), BF16),
        ],
        compiler_params=PARAMS,
        name="flow_products",
    )(me, flow, link, live, coefs, own, other)


def near_sum_kernel(me_ref, own_ref, a_ref, b_ref, mine_ref, next_a_ref, half_a_ref, half_b_ref, next_b_ref):
    group = me_ref[0] // 4
    groups = own_ref.shape[0] // 2
    forth = jnp.where(group % 2 == 0, 1, groups - 1)

    def total(steps, part):
        at = ((group + steps) % groups) * 2 + part
        return (
            own_ref[at].astype(F32) + a_ref[at].astype(F32) + b_ref[at].astype(F32)
        ).astype(BF16)

    for part in range(2):
        mine_ref[part] = total(0, part)
        next_a_ref[part] = total(forth, part)
        next_b_ref[part] = total(groups - forth, part)
    half_a_ref[0] = total(2, 0)
    half_b_ref[0] = total(2, 1)


def near_sum(me, own, a, b):
    counts = [2, 2, 1, 1, 2]
    return pl.pallas_call(
        near_sum_kernel,
        out_shape=[jax.ShapeDtypeStruct((count, BS, H), BF16) for count in counts],
        in_specs=[SMEM, VMEM, VMEM, VMEM],
        out_specs=[VMEM] * len(counts),
        compiler_params=PARAMS,
        name="near_sum",
    )(me, own, a, b)


def add(a, b):
    return (a.astype(F32) + b.astype(F32)).astype(BF16)


def pair_ring(next_a, half_a, half_b, next_b, swap_a, swap_b):
    cut = half_a.shape[0]
    got_a = lax.ppermute(half_a, "row", swap_a)
    got_b = lax.ppermute(half_b, "row", swap_b)
    next_b = jnp.concatenate([add(next_b[:cut], got_a), next_b[cut:]], axis=0)
    next_a = jnp.concatenate([next_a[:cut], add(next_a[cut:], got_b)], axis=0)
    got_b = lax.ppermute(next_b, "row", swap_b)
    got_a = lax.ppermute(next_a, "row", swap_a)
    return got_a, got_b


def sum_over_rows(me, own, near_a, half_a, half_b, near_b, rows):
    def swaps(step):
        return (
            [(i, i ^ step) for i in range(rows)],
            [(i, (((i - step) % rows) ^ step) + step) for i in range(rows)],
        )

    def wrap(pairs):
        return [(i, j % rows) for i, j in pairs]

    swap_a, swap_b = map(wrap, swaps(1))
    got_a, got_b = pair_ring(near_a, half_a, half_b, near_b, swap_a, swap_b)
    mine, far_a, half_a, half_b, far_b = near_sum(me, own, got_a, got_b)
    swap_a, swap_b = map(wrap, swaps(4))
    got_a, got_b = pair_ring(far_a, half_a, half_b, far_b, swap_a, swap_b)
    return jnp.stack([x.reshape(2 * BS, H) for x in (mine, got_a, got_b)])


def add_kernel(a_ref, b_ref, out_ref):
    out_ref[...] = (a_ref[...].astype(F32) + b_ref[...].astype(F32)).astype(BF16)


def add_two(a, b):
    return pl.pallas_call(
        add_kernel,
        out_shape=jax.ShapeDtypeStruct(a.shape, BF16),
        in_specs=[VMEM, VMEM],
        out_specs=VMEM,
        compiler_params=PARAMS,
        name="add_two",
    )(a, b)


def update_kernel(parts_ref, state_ref, gain_ref, agg_ref, self_ref, out_w_ref, *out_refs):
    totals = jnp.sum(parts_ref[...].astype(F32), axis=0)
    scale = lax.rsqrt(jnp.mean(totals * totals, axis=-1, keepdims=True) + 1e-05)
    normed = (totals * scale * gain_ref[...]).astype(BF16)
    before = jnp.dot(normed, agg_ref[...], preferred_element_type=F32) + jnp.dot(
        state_ref[...], self_ref[...], preferred_element_type=F32
    )
    hidden = jax.nn.silu(before).astype(BF16)
    result = (
        state_ref[...].astype(F32)
        + jnp.dot(hidden, out_w_ref[...], preferred_element_type=F32)
    ).astype(BF16)
    out_refs[0][...] = result
    if len(out_refs) > 1:
        for copy in range(out_refs[1].shape[0]):
            out_refs[1][copy] = result


def update(parts, state, gain, agg_weight, self_weight, out_weight, copies):
    shapes = [jax.ShapeDtypeStruct(state.shape, BF16)]
    if copies:
        shapes.append(jax.ShapeDtypeStruct((copies,) + state.shape, BF16))
    return pl.pallas_call(
        update_kernel,
        out_shape=shapes,
        in_specs=[VMEM] * 6,
        out_specs=[VMEM] * len(shapes),
        compiler_params=PARAMS,
        name="link_update" if copies else "flow_update",
    )(parts, state, gain.reshape(1, H), agg_weight, self_weight, out_weight)


def on_device(
    flow_state,
    link_state,
    incidence,
    tile_flow,
    tile_link,
    tile_live,
    link_gain,
    link_agg_weight,
    link_self_weight,
    link_out_weight,
    flow_gain,
    flow_agg_weight,
    flow_self_weight,
    flow_out_weight,
):
    coefs = incidence[0, 0]
    cols = lax.axis_size("col")
    rows = lax.axis_size("row")
    pairs = cols // 2
    flow_blocks = flow_state.shape[0] // BS * rows
    me = jnp.stack([lax.axis_index("row"), lax.axis_index("col") % 2]).astype(jnp.int32)
    sibling = [(i, i ^ 1) for i in range(cols)]
    same_core = [[2 * i + core for i in range(pairs)] for core in range(2)]

    flow_group = gather_rows(flow_state)
    own, other = link_products(
        me, tile_flow, tile_link, tile_live, coefs,
        flow_group.reshape(flow_blocks, BS, H), cols,
    )
    own = add_two(own, lax.ppermute(other, "col", sibling))
    link_parts = lax.all_to_all(own, "col", 0, 0, tiled=True, axis_index_groups=same_core)
    link_next, link_copies = update(
        link_parts, link_state, link_gain, link_agg_weight, link_self_weight, link_out_weight, pairs
    )
    own = lax.all_to_all(link_copies, "col", 0, 0, tiled=True, axis_index_groups=same_core)
    other = lax.ppermute(own, "col", sibling)
    parts = flow_products(
        me, tile_flow, tile_link, tile_live, coefs, own, other, flow_blocks
    )
    flow_parts = sum_over_rows(me, *parts, rows)
    (flow_next,) = update(
        flow_parts, flow_state, flow_gain, flow_agg_weight, flow_self_weight, flow_out_weight, 0
    )
    return (link_next, flow_next)


def gather_rows(state):
    sent = (state.astype(F32) * SCALE).astype(jnp.float16)
    got = lax.all_gather(sent, "row", axis=0, tiled=True)
    return (got.astype(F32) * (1 / SCALE)).astype(BF16)


def solution(mesh):
    return jax.shard_map(
        on_device,
        mesh=mesh,
        in_specs=(
            P(("col", "row"), None),
            P(("row", "col"), None),
            P("row", "col", None, None, None),
            P("row", "col", None),
            P("row", "col", None),
            P("row", "col", None),
            P(),
            P(),
            P(),
            P(),
            P(),
            P(),
            P(),
            P(),
        ),
        out_specs=(P(("row", "col"), None), P(("col", "row"), None)),
        check_vma=False,
    )
```

```python
import functools
import jax
import jax.numpy as jnp
from jax import lax
from jax.experimental import pallas as pl
from jax.experimental.pallas import tpu as pltpu
from jax.sharding import PartitionSpec as P

H = 256
BS = 128
VMEM = pl.BlockSpec(memory_space=pltpu.VMEM)
SMEM = pl.BlockSpec(memory_space=pltpu.SMEM)
PARAMS = pltpu.CompilerParams(vmem_limit_bytes=40 << 20)
F32 = jnp.float32
BF16 = jnp.bfloat16
SCALE = 8192.0


def link_products_kernel(
    me_ref, flow_ref, link_ref, live_ref, coefs_ref, pieces_ref, own_ref, other_ref, acc_ref
):
    blocks = acc_ref.shape[0] - 1
    half = blocks // 2
    acc_ref[...] = jnp.zeros_like(acc_ref)
    for slot in range(coefs_ref.shape[0]):
        block = link_ref[0, 0, slot]
        place = ((block + me_ref[1]) % 2) * half + block // 2
        place = jnp.where(live_ref[0, 0, slot] == 1, place, blocks)
        acc_ref[place] += lax.dot_general(
            coefs_ref[slot],
            pieces_ref[flow_ref[0, 0, slot]],
            (((0,), (0,)), ((), ())),
            preferred_element_type=F32,
        )
    own_ref[...] = acc_ref[:half].astype(BF16)
    other_ref[...] = acc_ref[half : 2 * half].astype(BF16)


def link_products(me, flow, link, live, coefs, pieces, blocks):
    shape = jax.ShapeDtypeStruct((blocks // 2, BS, H), BF16)
    return pl.pallas_call(
        link_products_kernel,
        out_shape=[shape, shape],
        in_specs=[SMEM, SMEM, SMEM, SMEM, VMEM, VMEM],
        out_specs=[VMEM, VMEM],
        scratch_shapes=[pltpu.VMEM((blocks + 1, BS, H), F32)],
        compiler_params=PARAMS,
        name="link_products",
    )(me, flow, link, live, coefs, pieces)


def flow_products_kernel(
    me_ref, flow_ref, link_ref, live_ref, coefs_ref, own_ref, other_ref, *rest
):
    *out_refs, acc_ref, pieces_ref = rest
    blocks = acc_ref.shape[0] - 1
    quarter = blocks // 4
    half = own_ref.shape[0]
    pieces_ref[:half] = own_ref[...]
    pieces_ref[half:] = other_ref[...]
    acc_ref[...] = jnp.zeros_like(acc_ref)
    for slot in range(coefs_ref.shape[0]):
        block = flow_ref[0, 0, slot]
        row = block // 2
        ahead = jnp.where(me_ref[0] % 2 == 0, row - me_ref[0], me_ref[0] - row)
        place = ((ahead + 2 * blocks) % 4) * quarter + (row // 4) * 2 + block % 2
        place = jnp.where(live_ref[0, 0, slot] == 1, place, blocks)
        piece = link_ref[0, 0, slot]
        piece = ((piece + me_ref[1]) % 2) * half + piece // 2
        acc_ref[place] += jnp.dot(
            coefs_ref[slot], pieces_ref[piece], preferred_element_type=F32
        )
    start = 0
    for out_ref in out_refs:
        count = out_ref.shape[0]
        out_ref[...] = acc_ref[start : start + count].astype(BF16)
        start += count


def flow_products(me, flow, link, live, coefs, own, other, blocks):
    counts = [blocks // 4, blocks // 4, blocks // 8, blocks // 8, blocks // 4]
    return pl.pallas_call(
        flow_products_kernel,
        out_shape=[jax.ShapeDtypeStruct((count, BS, H), BF16) for count in counts],
        in_specs=[SMEM, SMEM, SMEM, SMEM, VMEM, VMEM, VMEM],
        out_specs=[VMEM] * len(counts),
        scratch_shapes=[
            pltpu.VMEM((blocks + 1, BS, H), F32),
            pltpu.VMEM((2 * own.shape[0], BS, H), BF16),
        ],
        compiler_params=PARAMS,
        name="flow_products",
    )(me, flow, link, live, coefs, own, other)


def near_sum_kernel(me_ref, own_ref, a_ref, b_ref, mine_ref, next_a_ref, half_a_ref, half_b_ref, next_b_ref):
    group = me_ref[0] // 4
    groups = own_ref.shape[0] // 2
    forth = jnp.where(group % 2 == 0, 1, groups - 1)

    def total(steps, part):
        at = ((group + steps) % groups) * 2 + part
        return (
            own_ref[at].astype(F32) + a_ref[at].astype(F32) + b_ref[at].astype(F32)
        ).astype(BF16)

    for part in range(2):
        mine_ref[part] = total(0, part)
        next_a_ref[part] = total(forth, part)
        next_b_ref[part] = total(groups - forth, part)
    half_a_ref[0] = total(2, 0)
    half_b_ref[0] = total(2, 1)


def near_sum(me, own, a, b):
    counts = [2, 2, 1, 1, 2]
    return pl.pallas_call(
        near_sum_kernel,
        out_shape=[jax.ShapeDtypeStruct((count, BS, H), BF16) for count in counts],
        in_specs=[SMEM, VMEM, VMEM, VMEM],
        out_specs=[VMEM] * len(counts),
        compiler_params=PARAMS,
        name="near_sum",
    )(me, own, a, b)


def add(a, b):
    return (a.astype(F32) + b.astype(F32)).astype(BF16)


def pair_ring(next_a, half_a, half_b, next_b, swap_a, swap_b):
    cut = half_a.shape[0]
    got_a = lax.ppermute(half_a, "row", swap_a)
    got_b = lax.ppermute(half_b, "row", swap_b)
    plain_a = lax.ppermute(next_a[:cut], "row", swap_a)
    plain_b = lax.ppermute(next_b[cut:], "row", swap_b)
    summed_b = lax.ppermute(add(next_b[:cut], got_a), "row", swap_b)
    summed_a = lax.ppermute(add(next_a[cut:], got_b), "row", swap_a)
    return (
        jnp.concatenate([plain_a, summed_a], axis=0),
        jnp.concatenate([summed_b, plain_b], axis=0),
    )


def sum_over_rows(me, own, near_a, half_a, half_b, near_b, rows):
    def swaps(step):
        return (
            [(i, i ^ step) for i in range(rows)],
            [(i, (((i - step) % rows) ^ step) + step) for i in range(rows)],
        )

    def wrap(pairs):
        return [(i, j % rows) for i, j in pairs]

    swap_a, swap_b = map(wrap, swaps(1))
    got_a, got_b = pair_ring(near_a, half_a, half_b, near_b, swap_a, swap_b)
    mine, far_a, half_a, half_b, far_b = near_sum(me, own, got_a, got_b)
    swap_a, swap_b = map(wrap, swaps(4))
    got_a, got_b = pair_ring(far_a, half_a, half_b, far_b, swap_a, swap_b)
    return jnp.stack([x.reshape(2 * BS, H) for x in (mine, got_a, got_b)])


def add_kernel(a_ref, b_ref, out_ref):
    out_ref[...] = (a_ref[...].astype(F32) + b_ref[...].astype(F32)).astype(BF16)


def add_two(a, b):
    return pl.pallas_call(
        add_kernel,
        out_shape=jax.ShapeDtypeStruct(a.shape, BF16),
        in_specs=[VMEM, VMEM],
        out_specs=VMEM,
        compiler_params=PARAMS,
        name="add_two",
    )(a, b)


def update_kernel(parts_ref, state_ref, gain_ref, agg_ref, self_ref, out_w_ref, *out_refs):
    totals = jnp.sum(parts_ref[...].astype(F32), axis=0)
    scale = lax.rsqrt(jnp.mean(totals * totals, axis=-1, keepdims=True) + 1e-05)
    normed = (totals * scale * gain_ref[...]).astype(BF16)
    before = jnp.dot(normed, agg_ref[...], preferred_element_type=F32) + jnp.dot(
        state_ref[...], self_ref[...], preferred_element_type=F32
    )
    hidden = jax.nn.silu(before).astype(BF16)
    result = (
        state_ref[...].astype(F32)
        + jnp.dot(hidden, out_w_ref[...], preferred_element_type=F32)
    ).astype(BF16)
    out_refs[0][...] = result
    if len(out_refs) > 1:
        for copy in range(out_refs[1].shape[0]):
            out_refs[1][copy] = result


def update(parts, state, gain, agg_weight, self_weight, out_weight, copies):
    shapes = [jax.ShapeDtypeStruct(state.shape, BF16)]
    if copies:
        shapes.append(jax.ShapeDtypeStruct((copies,) + state.shape, BF16))
    return pl.pallas_call(
        update_kernel,
        out_shape=shapes,
        in_specs=[VMEM] * 6,
        out_specs=[VMEM] * len(shapes),
        compiler_params=PARAMS,
        name="link_update" if copies else "flow_update",
    )(parts, state, gain.reshape(1, H), agg_weight, self_weight, out_weight)


def on_device(
    flow_state,
    link_state,
    incidence,
    tile_flow,
    tile_link,
    tile_live,
    link_gain,
    link_agg_weight,
    link_self_weight,
    link_out_weight,
    flow_gain,
    flow_agg_weight,
    flow_self_weight,
    flow_out_weight,
):
    coefs = incidence[0, 0]
    cols = lax.axis_size("col")
    rows = lax.axis_size("row")
    pairs = cols // 2
    flow_blocks = flow_state.shape[0] // BS * rows
    me = jnp.stack([lax.axis_index("row"), lax.axis_index("col") % 2]).astype(jnp.int32)
    sibling = [(i, i ^ 1) for i in range(cols)]
    same_core = [[2 * i + core for i in range(pairs)] for core in range(2)]

    flow_group = gather_rows(flow_state)
    own, other = link_products(
        me, tile_flow, tile_link, tile_live, coefs,
        flow_group.reshape(flow_blocks, BS, H), cols,
    )
    own = add_two(own, lax.ppermute(other, "col", sibling))
    link_parts = lax.all_to_all(own, "col", 0, 0, tiled=True, axis_index_groups=same_core)
    link_next, link_copies = update(
        link_parts, link_state, link_gain, link_agg_weight, link_self_weight, link_out_weight, pairs
    )
    own = lax.all_to_all(link_copies, "col", 0, 0, tiled=True, axis_index_groups=same_core)
    other = lax.ppermute(own, "col", sibling)
    parts = flow_products(
        me, tile_flow, tile_link, tile_live, coefs, own, other, flow_blocks
    )
    flow_parts = sum_over_rows(me, *parts, rows)
    (flow_next,) = update(
        flow_parts, flow_state, flow_gain, flow_agg_weight, flow_self_weight, flow_out_weight, 0
    )
    return (link_next, flow_next)


def gather_rows(state):
    sent = (state.astype(F32) * SCALE).astype(jnp.float16)
    got = lax.all_gather(sent, "row", axis=0, tiled=True)
    return (got.astype(F32) * (1 / SCALE)).astype(BF16)


def solution(mesh):
    return jax.shard_map(
        on_device,
        mesh=mesh,
        in_specs=(
            P(("col", "row"), None),
            P(("row", "col"), None),
            P("row", "col", None, None, None),
            P("row", "col", None),
            P("row", "col", None),
            P("row", "col", None),
            P(),
            P(),
            P(),
            P(),
            P(),
            P(),
            P(),
            P(),
        ),
        out_specs=(P(("row", "col"), None), P(("col", "row"), None)),
        check_vma=False,
    )
```

```python
import functools
import jax
import jax.numpy as jnp
from jax import lax
from jax.experimental import pallas as pl
from jax.experimental.pallas import tpu as pltpu
from jax.sharding import PartitionSpec as P

H = 256
BS = 128
VMEM = pl.BlockSpec(memory_space=pltpu.VMEM)
SMEM = pl.BlockSpec(memory_space=pltpu.SMEM)
PARAMS = pltpu.CompilerParams(vmem_limit_bytes=40 << 20)
F32 = jnp.float32
BF16 = jnp.bfloat16
SCALE = 8192.0


def link_products_kernel(
    me_ref, flow_ref, link_ref, live_ref, coefs_ref, pieces_ref, own_ref, other_ref, acc_ref
):
    blocks = acc_ref.shape[0] - 1
    half = blocks // 2
    acc_ref[...] = jnp.zeros_like(acc_ref)
    for slot in range(coefs_ref.shape[0]):
        block = link_ref[0, 0, slot]
        place = ((block + me_ref[1]) % 2) * half + block // 2
        place = jnp.where(live_ref[0, 0, slot] == 1, place, blocks)
        acc_ref[place] += lax.dot_general(
            coefs_ref[slot],
            pieces_ref[flow_ref[0, 0, slot]],
            (((0,), (0,)), ((), ())),
            preferred_element_type=F32,
        )
    own_ref[...] = acc_ref[:half].astype(BF16)
    other_ref[...] = acc_ref[half : 2 * half].astype(BF16)


def link_products(me, flow, link, live, coefs, pieces, blocks):
    shape = jax.ShapeDtypeStruct((blocks // 2, BS, H), BF16)
    return pl.pallas_call(
        link_products_kernel,
        out_shape=[shape, shape],
        in_specs=[SMEM, SMEM, SMEM, SMEM, VMEM, VMEM],
        out_specs=[VMEM, VMEM],
        scratch_shapes=[pltpu.VMEM((blocks + 1, BS, H), F32)],
        compiler_params=PARAMS,
        name="link_products",
    )(me, flow, link, live, coefs, pieces)


ROW_ORDER = (0, 5, -5, 2, 7, -3, -2, -7, 3, 1, 6, -4, -1, -6, 4, 8)


def flow_products_kernel(
    me_ref, flow_ref, link_ref, live_ref, coefs_ref, own_ref, other_ref, *rest
):
    *out_refs, acc_ref, pieces_ref, order_ref = rest
    blocks = acc_ref.shape[0] - 1
    rows = blocks // 2
    half = own_ref.shape[0]
    for place, ahead in enumerate(ROW_ORDER):
        order_ref[ahead % rows] = 2 * place
    pieces_ref[:half] = own_ref[...]
    pieces_ref[half:] = other_ref[...]
    acc_ref[...] = jnp.zeros_like(acc_ref)
    for slot in range(coefs_ref.shape[0]):
        block = flow_ref[0, 0, slot]
        ahead = jnp.where(me_ref[0] % 2 == 0, block // 2 - me_ref[0], me_ref[0] - block // 2)
        place = order_ref[(ahead + rows) % rows] + block % 2
        place = jnp.where(live_ref[0, 0, slot] == 1, place, blocks)
        piece = link_ref[0, 0, slot]
        piece = ((piece + me_ref[1]) % 2) * half + piece // 2
        acc_ref[place] += jnp.dot(
            coefs_ref[slot], pieces_ref[piece], preferred_element_type=F32
        )
    start = 0
    for out_ref in out_refs:
        count = out_ref.shape[0]
        out_ref[...] = acc_ref[start : start + count].astype(BF16)
        start += count


def flow_products(me, flow, link, live, coefs, own, other, blocks):
    assert blocks == 2 * len(ROW_ORDER)
    counts = [6] * 5 + [1, 1]
    return pl.pallas_call(
        flow_products_kernel,
        out_shape=[jax.ShapeDtypeStruct((count, BS, H), BF16) for count in counts],
        in_specs=[SMEM, SMEM, SMEM, SMEM, VMEM, VMEM, VMEM],
        out_specs=[VMEM] * len(counts),
        scratch_shapes=[
            pltpu.VMEM((blocks + 1, BS, H), F32),
            pltpu.VMEM((2 * own.shape[0], BS, H), BF16),
            pltpu.SMEM((len(ROW_ORDER),), jnp.int32),
        ],
        compiler_params=PARAMS,
        name="flow_products",
    )(me, flow, link, live, coefs, own, other)


def add(*terms):
    total = terms[0].astype(F32)
    for term in terms[1:]:
        total = total + term.astype(F32)
    return total.astype(BF16)


def sum_over_rows(own, two_a, two_b, one_a, one_b, opposite_a, opposite_b, rows):
    def swap_a(x, step):
        pairs = [(i, (i + step if i % 2 == 0 else i - step) % rows) for i in range(rows)]
        return lax.ppermute(x, "row", pairs)

    def swap_b(x, step):
        pairs = [(i, (i - step if i % 2 == 0 else i + step) % rows) for i in range(rows)]
        return lax.ppermute(x, "row", pairs)

    got_a, got_b = swap_a(two_a, 1), swap_b(two_b, 1)
    from_a, from_b = swap_a(opposite_a, 3), swap_b(opposite_b, 3)
    one_b, one_a = add(one_b, got_a), add(one_a, got_b)
    got_a, got_b = swap_a(one_a, 1), swap_b(one_b, 1)
    mine = add(own[:2], got_a[:2], got_b[:2])
    far_a = jnp.concatenate(
        [add(own[2:3], got_a[4:5], got_b[2:3]), add(own[3:4], got_a[5:6], got_b[3:4], from_b)], axis=0
    )
    far_b = jnp.concatenate(
        [add(own[4:5], got_a[2:3], got_b[4:5], from_a), add(own[5:6], got_a[3:4], got_b[5:6])], axis=0
    )
    got_a, got_b = swap_a(far_a, 5), swap_b(far_b, 5)
    return jnp.stack([x.reshape(2 * BS, H) for x in (mine, got_a, got_b)])


def add_kernel(a_ref, b_ref, out_ref):
    out_ref[...] = (a_ref[...].astype(F32) + b_ref[...].astype(F32)).astype(BF16)


def add_two(a, b):
    return pl.pallas_call(
        add_kernel,
        out_shape=jax.ShapeDtypeStruct(a.shape, BF16),
        in_specs=[VMEM, VMEM],
        out_specs=VMEM,
        compiler_params=PARAMS,
        name="add_two",
    )(a, b)


def update_kernel(parts_ref, state_ref, gain_ref, agg_ref, self_ref, out_w_ref, *out_refs):
    totals = jnp.sum(parts_ref[...].astype(F32), axis=0)
    scale = lax.rsqrt(jnp.mean(totals * totals, axis=-1, keepdims=True) + 1e-05)
    normed = (totals * scale * gain_ref[...]).astype(BF16)
    before = jnp.dot(normed, agg_ref[...], preferred_element_type=F32) + jnp.dot(
        state_ref[...], self_ref[...], preferred_element_type=F32
    )
    hidden = jax.nn.silu(before).astype(BF16)
    result = (
        state_ref[...].astype(F32)
        + jnp.dot(hidden, out_w_ref[...], preferred_element_type=F32)
    ).astype(BF16)
    out_refs[0][...] = result
    if len(out_refs) > 1:
        for copy in range(out_refs[1].shape[0]):
            out_refs[1][copy] = result


def update(parts, state, gain, agg_weight, self_weight, out_weight, copies):
    shapes = [jax.ShapeDtypeStruct(state.shape, BF16)]
    if copies:
        shapes.append(jax.ShapeDtypeStruct((copies,) + state.shape, BF16))
    return pl.pallas_call(
        update_kernel,
        out_shape=shapes,
        in_specs=[VMEM] * 6,
        out_specs=[VMEM] * len(shapes),
        compiler_params=PARAMS,
        name="link_update" if copies else "flow_update",
    )(parts, state, gain.reshape(1, H), agg_weight, self_weight, out_weight)


def on_device(
    flow_state,
    link_state,
    incidence,
    tile_flow,
    tile_link,
    tile_live,
    link_gain,
    link_agg_weight,
    link_self_weight,
    link_out_weight,
    flow_gain,
    flow_agg_weight,
    flow_self_weight,
    flow_out_weight,
):
    coefs = incidence[0, 0]
    cols = lax.axis_size("col")
    rows = lax.axis_size("row")
    pairs = cols // 2
    flow_blocks = flow_state.shape[0] // BS * rows
    me = jnp.stack([lax.axis_index("row"), lax.axis_index("col") % 2]).astype(jnp.int32)
    sibling = [(i, i ^ 1) for i in range(cols)]
    same_core = [[2 * i + core for i in range(pairs)] for core in range(2)]

    flow_group = gather_rows(flow_state)
    own, other = link_products(
        me, tile_flow, tile_link, tile_live, coefs,
        flow_group.reshape(flow_blocks, BS, H), cols,
    )
    own = add_two(own, lax.ppermute(other, "col", sibling))
    link_parts = lax.all_to_all(own, "col", 0, 0, tiled=True, axis_index_groups=same_core)
    link_next, link_copies = update(
        link_parts, link_state, link_gain, link_agg_weight, link_self_weight, link_out_weight, pairs
    )
    own = lax.all_to_all(link_copies, "col", 0, 0, tiled=True, axis_index_groups=same_core)
    other = lax.ppermute(own, "col", sibling)
    parts = flow_products(
        me, tile_flow, tile_link, tile_live, coefs, own, other, flow_blocks
    )
    flow_parts = sum_over_rows(*parts, rows)
    (flow_next,) = update(
        flow_parts, flow_state, flow_gain, flow_agg_weight, flow_self_weight, flow_out_weight, 0
    )
    return (link_next, flow_next)


def gather_rows(state):
    sent = (state.astype(F32) * SCALE).astype(jnp.float16)
    got = lax.all_gather(sent, "row", axis=0, tiled=True)
    return (got.astype(F32) * (1 / SCALE)).astype(BF16)


def solution(mesh):
    return jax.shard_map(
        on_device,
        mesh=mesh,
        in_specs=(
            P(("col", "row"), None),
            P(("row", "col"), None),
            P("row", "col", None, None, None),
            P("row", "col", None),
            P("row", "col", None),
            P("row", "col", None),
            P(),
            P(),
            P(),
            P(),
            P(),
            P(),
            P(),
            P(),
        ),
        out_specs=(P(("row", "col"), None), P(("col", "row"), None)),
        check_vma=False,
    )
```

```python
import functools
import jax
import jax.numpy as jnp
from jax import lax
from jax.experimental import pallas as pl
from jax.experimental.pallas import tpu as pltpu
from jax.sharding import PartitionSpec as P

H = 256
BS = 128
VMEM = pl.BlockSpec(memory_space=pltpu.VMEM)
SMEM = pl.BlockSpec(memory_space=pltpu.SMEM)
PARAMS = pltpu.CompilerParams(vmem_limit_bytes=40 << 20)
F32 = jnp.float32
BF16 = jnp.bfloat16
SCALE = 8192.0


def link_products_kernel(
    me_ref, flow_ref, link_ref, live_ref, coefs_ref, pieces_ref, own_ref, other_ref, acc_ref
):
    blocks = acc_ref.shape[0] - 1
    half = blocks // 2
    acc_ref[...] = jnp.zeros_like(acc_ref)
    for slot in range(coefs_ref.shape[0]):
        block = link_ref[0, 0, slot]
        place = ((block + me_ref[1]) % 2) * half + block // 2
        place = jnp.where(live_ref[0, 0, slot] == 1, place, blocks)
        acc_ref[place] += lax.dot_general(
            coefs_ref[slot],
            pieces_ref[flow_ref[0, 0, slot]],
            (((0,), (0,)), ((), ())),
            preferred_element_type=F32,
        )
    own_ref[...] = acc_ref[:half].astype(BF16)
    other_ref[...] = acc_ref[half : 2 * half].astype(BF16)


def link_products(me, flow, link, live, coefs, pieces, blocks):
    shape = jax.ShapeDtypeStruct((blocks // 2, BS, H), BF16)
    return pl.pallas_call(
        link_products_kernel,
        out_shape=[shape, shape],
        in_specs=[SMEM, SMEM, SMEM, SMEM, VMEM, VMEM],
        out_specs=[VMEM, VMEM],
        scratch_shapes=[pltpu.VMEM((blocks + 1, BS, H), F32)],
        compiler_params=PARAMS,
        name="link_products",
    )(me, flow, link, live, coefs, pieces)


ROW_ORDER = (0, 5, -5, 2, 7, -3, -2, -7, 3, 1, 6, -4, -1, -6, 4, 8)


def flow_products_kernel(
    me_ref, flow_ref, link_ref, live_ref, coefs_ref, own_ref, other_ref, *rest
):
    *out_refs, acc_ref, pieces_ref, order_ref = rest
    blocks = acc_ref.shape[0] - 1
    rows = blocks // 2
    half = own_ref.shape[0]
    for place, ahead in enumerate(ROW_ORDER):
        order_ref[ahead % rows] = 2 * place
    pieces_ref[:half] = own_ref[...]
    pieces_ref[half:] = other_ref[...]
    acc_ref[...] = jnp.zeros_like(acc_ref)
    for slot in range(coefs_ref.shape[0]):
        block = flow_ref[0, 0, slot]
        ahead = jnp.where(me_ref[0] % 2 == 0, block // 2 - me_ref[0], me_ref[0] - block // 2)
        place = order_ref[(ahead + rows) % rows] + block % 2
        place = jnp.where(live_ref[0, 0, slot] == 1, place, blocks)
        piece = link_ref[0, 0, slot]
        piece = ((piece + me_ref[1]) % 2) * half + piece // 2
        acc_ref[place] += jnp.dot(
            coefs_ref[slot], pieces_ref[piece], preferred_element_type=F32
        )
    start = 0
    for out_ref in out_refs:
        count = out_ref.shape[0]
        out_ref[...] = acc_ref[start : start + count].astype(BF16)
        start += count


def flow_products(me, flow, link, live, coefs, own, other, blocks):
    assert blocks == 2 * len(ROW_ORDER)
    counts = [6] * 5 + [2]
    return pl.pallas_call(
        flow_products_kernel,
        out_shape=[jax.ShapeDtypeStruct((count, BS, H), BF16) for count in counts],
        in_specs=[SMEM, SMEM, SMEM, SMEM, VMEM, VMEM, VMEM],
        out_specs=[VMEM] * len(counts),
        scratch_shapes=[
            pltpu.VMEM((blocks + 1, BS, H), F32),
            pltpu.VMEM((2 * own.shape[0], BS, H), BF16),
            pltpu.SMEM((len(ROW_ORDER),), jnp.int32),
        ],
        compiler_params=PARAMS,
        name="flow_products",
    )(me, flow, link, live, coefs, own, other)


def add(*terms):
    total = terms[0].astype(F32)
    for term in terms[1:]:
        total = total + term.astype(F32)
    return total.astype(BF16)


def sum_over_rows(own, two_a, two_b, one_a, one_b, opposite, rows):
    def swap_a(x, step):
        pairs = [(i, (i + step if i % 2 == 0 else i - step) % rows) for i in range(rows)]
        return lax.ppermute(x, "row", pairs)

    def swap_b(x, step):
        pairs = [(i, (i - step if i % 2 == 0 else i + step) % rows) for i in range(rows)]
        return lax.ppermute(x, "row", pairs)

    got_a, got_b = swap_a(two_a, 1), swap_b(two_b, 1)
    opposite = swap_a(opposite, 3)
    got_a, got_b, opposite = lax.optimization_barrier((got_a, got_b, opposite))
    one_b, one_a = add(one_b, got_a), add(one_a, got_b)
    got_a, got_b = swap_a(one_a, 1), swap_b(one_b, 1)
    mine = add(own[:2], got_a[:2], got_b[:2])
    far_a = add(own[2:4], got_a[4:6], got_b[2:4])
    far_b = add(own[4:6], got_a[2:4], got_b[4:6], opposite)
    got_a, got_b = swap_a(far_a, 5), swap_b(far_b, 5)
    return jnp.stack([x.reshape(2 * BS, H) for x in (mine, got_a, got_b)])


def add_kernel(a_ref, b_ref, out_ref):
    out_ref[...] = (a_ref[...].astype(F32) + b_ref[...].astype(F32)).astype(BF16)


def add_two(a, b):
    return pl.pallas_call(
        add_kernel,
        out_shape=jax.ShapeDtypeStruct(a.shape, BF16),
        in_specs=[VMEM, VMEM],
        out_specs=VMEM,
        compiler_params=PARAMS,
        name="add_two",
    )(a, b)


def update_kernel(parts_ref, state_ref, gain_ref, agg_ref, self_ref, out_w_ref, *out_refs):
    totals = jnp.sum(parts_ref[...].astype(F32), axis=0)
    scale = lax.rsqrt(jnp.mean(totals * totals, axis=-1, keepdims=True) + 1e-05)
    normed = (totals * scale * gain_ref[...]).astype(BF16)
    before = jnp.dot(normed, agg_ref[...], preferred_element_type=F32) + jnp.dot(
        state_ref[...], self_ref[...], preferred_element_type=F32
    )
    hidden = jax.nn.silu(before).astype(BF16)
    result = (
        state_ref[...].astype(F32)
        + jnp.dot(hidden, out_w_ref[...], preferred_element_type=F32)
    ).astype(BF16)
    out_refs[0][...] = result
    if len(out_refs) > 1:
        for copy in range(out_refs[1].shape[0]):
            out_refs[1][copy] = result


def update(parts, state, gain, agg_weight, self_weight, out_weight, copies):
    shapes = [jax.ShapeDtypeStruct(state.shape, BF16)]
    if copies:
        shapes.append(jax.ShapeDtypeStruct((copies,) + state.shape, BF16))
    return pl.pallas_call(
        update_kernel,
        out_shape=shapes,
        in_specs=[VMEM] * 6,
        out_specs=[VMEM] * len(shapes),
        compiler_params=PARAMS,
        name="link_update" if copies else "flow_update",
    )(parts, state, gain.reshape(1, H), agg_weight, self_weight, out_weight)


def on_device(
    flow_state,
    link_state,
    incidence,
    tile_flow,
    tile_link,
    tile_live,
    link_gain,
    link_agg_weight,
    link_self_weight,
    link_out_weight,
    flow_gain,
    flow_agg_weight,
    flow_self_weight,
    flow_out_weight,
):
    coefs = incidence[0, 0]
    cols = lax.axis_size("col")
    rows = lax.axis_size("row")
    pairs = cols // 2
    flow_blocks = flow_state.shape[0] // BS * rows
    me = jnp.stack([lax.axis_index("row"), lax.axis_index("col") % 2]).astype(jnp.int32)
    sibling = [(i, i ^ 1) for i in range(cols)]
    same_core = [[2 * i + core for i in range(pairs)] for core in range(2)]

    flow_group = gather_rows(flow_state)
    own, other = link_products(
        me, tile_flow, tile_link, tile_live, coefs,
        flow_group.reshape(flow_blocks, BS, H), cols,
    )
    own = add_two(own, lax.ppermute(other, "col", sibling))
    link_parts = lax.all_to_all(own, "col", 0, 0, tiled=True, axis_index_groups=same_core)
    link_next, link_copies = update(
        link_parts, link_state, link_gain, link_agg_weight, link_self_weight, link_out_weight, pairs
    )
    own = lax.all_to_all(link_copies, "col", 0, 0, tiled=True, axis_index_groups=same_core)
    other = lax.ppermute(own, "col", sibling)
    parts = flow_products(
        me, tile_flow, tile_link, tile_live, coefs, own, other, flow_blocks
    )
    flow_parts = sum_over_rows(*parts, rows)
    (flow_next,) = update(
        flow_parts, flow_state, flow_gain, flow_agg_weight, flow_self_weight, flow_out_weight, 0
    )
    return (link_next, flow_next)


def gather_rows(state):
    sent = (state.astype(F32) * SCALE).astype(jnp.float16)
    got = lax.all_gather(sent, "row", axis=0, tiled=True)
    return (got.astype(F32) * (1 / SCALE)).astype(BF16)


def solution(mesh):
    return jax.shard_map(
        on_device,
        mesh=mesh,
        in_specs=(
            P(("col", "row"), None),
            P(("row", "col"), None),
            P("row", "col", None, None, None),
            P("row", "col", None),
            P("row", "col", None),
            P("row", "col", None),
            P(),
            P(),
            P(),
            P(),
            P(),
            P(),
            P(),
            P(),
        ),
        out_specs=(P(("row", "col"), None), P(("col", "row"), None)),
        check_vma=False,
    )
```

```python
import functools
import jax
import jax.numpy as jnp
from jax import lax
from jax.experimental import pallas as pl
from jax.experimental.pallas import tpu as pltpu
from jax.sharding import PartitionSpec as P

H = 256
BS = 128
VMEM = pl.BlockSpec(memory_space=pltpu.VMEM)
SMEM = pl.BlockSpec(memory_space=pltpu.SMEM)
PARAMS = pltpu.CompilerParams(vmem_limit_bytes=40 << 20)
F32 = jnp.float32
BF16 = jnp.bfloat16
SCALE = 8192.0


def link_products_kernel(
    me_ref, flow_ref, link_ref, live_ref, coefs_ref, pieces_ref, own_ref, other_ref, acc_ref
):
    blocks = acc_ref.shape[0] - 1
    half = blocks // 2
    acc_ref[...] = jnp.zeros_like(acc_ref)
    for slot in range(coefs_ref.shape[0]):
        block = link_ref[0, 0, slot]
        place = ((block + me_ref[1]) % 2) * half + block // 2
        place = jnp.where(live_ref[0, 0, slot] == 1, place, blocks)
        acc_ref[place] += lax.dot_general(
            coefs_ref[slot],
            pieces_ref[flow_ref[0, 0, slot]],
            (((0,), (0,)), ((), ())),
            preferred_element_type=F32,
        )
    own_ref[...] = acc_ref[:half].astype(BF16)
    other_ref[...] = acc_ref[half : 2 * half].astype(BF16)


def link_products(me, flow, link, live, coefs, pieces, blocks):
    shape = jax.ShapeDtypeStruct((blocks // 2, BS, H), BF16)
    return pl.pallas_call(
        link_products_kernel,
        out_shape=[shape, shape],
        in_specs=[SMEM, SMEM, SMEM, SMEM, VMEM, VMEM],
        out_specs=[VMEM, VMEM],
        scratch_shapes=[pltpu.VMEM((blocks + 1, BS, H), F32)],
        compiler_params=PARAMS,
        name="link_products",
    )(me, flow, link, live, coefs, pieces)


ROW_ORDER = (0, 5, -5, 2, 7, -3, -2, -7, 3, 1, 6, -4, -1, -6, 4, 8)


def flow_products_kernel(
    me_ref, flow_ref, link_ref, live_ref, coefs_ref, own_ref, other_ref, *rest
):
    *out_refs, acc_ref, pieces_ref, order_ref = rest
    blocks = acc_ref.shape[0] - 1
    rows = blocks // 2
    half = own_ref.shape[0]
    for place, ahead in enumerate(ROW_ORDER):
        order_ref[ahead % rows] = 2 * place
    pieces_ref[:half] = own_ref[...]
    pieces_ref[half:] = other_ref[...]
    acc_ref[...] = jnp.zeros_like(acc_ref)
    for slot in range(coefs_ref.shape[0]):
        block = flow_ref[0, 0, slot]
        ahead = jnp.where(me_ref[0] % 2 == 0, block // 2 - me_ref[0], me_ref[0] - block // 2)
        place = order_ref[(ahead + rows) % rows] + block % 2
        place = jnp.where(live_ref[0, 0, slot] == 1, place, blocks)
        piece = link_ref[0, 0, slot]
        piece = ((piece + me_ref[1]) % 2) * half + piece // 2
        acc_ref[place] += jnp.dot(
            coefs_ref[slot], pieces_ref[piece], preferred_element_type=F32
        )
    start = 0
    for out_ref in out_refs:
        count = out_ref.shape[0]
        out_ref[...] = acc_ref[start : start + count].astype(BF16)
        start += count


def flow_products(me, flow, link, live, coefs, own, other, blocks):
    assert blocks == 2 * len(ROW_ORDER)
    counts = [6] + [3] * 8 + [2]
    return pl.pallas_call(
        flow_products_kernel,
        out_shape=[jax.ShapeDtypeStruct((count, BS, H), BF16) for count in counts],
        in_specs=[SMEM, SMEM, SMEM, SMEM, VMEM, VMEM, VMEM],
        out_specs=[VMEM] * len(counts),
        scratch_shapes=[
            pltpu.VMEM((blocks + 1, BS, H), F32),
            pltpu.VMEM((2 * own.shape[0], BS, H), BF16),
            pltpu.SMEM((len(ROW_ORDER),), jnp.int32),
        ],
        compiler_params=PARAMS,
        name="flow_products",
    )(me, flow, link, live, coefs, own, other)


def add(*terms):
    total = terms[0].astype(F32)
    for term in terms[1:]:
        total = total + term.astype(F32)
    return total.astype(BF16)


def sum_over_rows(own, *parts):
    *two_a, two_b0, two_b1, one_a0, one_a1, one_b0, one_b1, opposite = parts
    rows = len(ROW_ORDER)

    def swap_a(x, step):
        pairs = [(i, (i + step if i % 2 == 0 else i - step) % rows) for i in range(rows)]
        return lax.ppermute(x, "row", pairs)

    def swap_b(x, step):
        pairs = [(i, (i - step if i % 2 == 0 else i + step) % rows) for i in range(rows)]
        return lax.ppermute(x, "row", pairs)

    halves_a, halves_b = [], []
    for half_a, half_b, next_a, next_b in zip(
        two_a, (two_b0, two_b1), (one_a0, one_a1), (one_b0, one_b1)
    ):
        got_a, got_b = swap_a(half_a, 1), swap_b(half_b, 1)
        halves_b.append(swap_b(add(next_b, got_a), 1))
        halves_a.append(swap_a(add(next_a, got_b), 1))
    opposite = swap_a(opposite, 3)
    got_a, got_b = jnp.concatenate(halves_a, axis=0), jnp.concatenate(halves_b, axis=0)
    mine = add(own[:2], got_a[:2], got_b[:2])
    far_a = add(own[2:4], got_a[4:6], got_b[2:4])
    far_b = add(own[4:6], got_a[2:4], got_b[4:6], opposite)
    got_a, got_b = swap_a(far_a, 5), swap_b(far_b, 5)
    return jnp.stack([x.reshape(2 * BS, H) for x in (mine, got_a, got_b)])


def add_kernel(a_ref, b_ref, out_ref):
    out_ref[...] = (a_ref[...].astype(F32) + b_ref[...].astype(F32)).astype(BF16)


def add_two(a, b):
    return pl.pallas_call(
        add_kernel,
        out_shape=jax.ShapeDtypeStruct(a.shape, BF16),
        in_specs=[VMEM, VMEM],
        out_specs=VMEM,
        compiler_params=PARAMS,
        name="add_two",
    )(a, b)


def update_kernel(parts_ref, state_ref, gain_ref, agg_ref, self_ref, out_w_ref, *out_refs):
    totals = jnp.sum(parts_ref[...].astype(F32), axis=0)
    scale = lax.rsqrt(jnp.mean(totals * totals, axis=-1, keepdims=True) + 1e-05)
    normed = (totals * scale * gain_ref[...]).astype(BF16)
    before = jnp.dot(normed, agg_ref[...], preferred_element_type=F32) + jnp.dot(
        state_ref[...], self_ref[...], preferred_element_type=F32
    )
    hidden = jax.nn.silu(before).astype(BF16)
    result = (
        state_ref[...].astype(F32)
        + jnp.dot(hidden, out_w_ref[...], preferred_element_type=F32)
    ).astype(BF16)
    out_refs[0][...] = result
    if len(out_refs) > 1:
        for copy in range(out_refs[1].shape[0]):
            out_refs[1][copy] = result


def update(parts, state, gain, agg_weight, self_weight, out_weight, copies):
    shapes = [jax.ShapeDtypeStruct(state.shape, BF16)]
    if copies:
        shapes.append(jax.ShapeDtypeStruct((copies,) + state.shape, BF16))
    return pl.pallas_call(
        update_kernel,
        out_shape=shapes,
        in_specs=[VMEM] * 6,
        out_specs=[VMEM] * len(shapes),
        compiler_params=PARAMS,
        name="link_update" if copies else "flow_update",
    )(parts, state, gain.reshape(1, H), agg_weight, self_weight, out_weight)


def on_device(
    flow_state,
    link_state,
    incidence,
    tile_flow,
    tile_link,
    tile_live,
    link_gain,
    link_agg_weight,
    link_self_weight,
    link_out_weight,
    flow_gain,
    flow_agg_weight,
    flow_self_weight,
    flow_out_weight,
):
    coefs = incidence[0, 0]
    cols = lax.axis_size("col")
    rows = lax.axis_size("row")
    pairs = cols // 2
    flow_blocks = flow_state.shape[0] // BS * rows
    me = jnp.stack([lax.axis_index("row"), lax.axis_index("col") % 2]).astype(jnp.int32)
    sibling = [(i, i ^ 1) for i in range(cols)]
    same_core = [[2 * i + core for i in range(pairs)] for core in range(2)]

    flow_group = gather_rows(flow_state)
    own, other = link_products(
        me, tile_flow, tile_link, tile_live, coefs,
        flow_group.reshape(flow_blocks, BS, H), cols,
    )
    own = add_two(own, lax.ppermute(other, "col", sibling))
    link_parts = lax.all_to_all(own, "col", 0, 0, tiled=True, axis_index_groups=same_core)
    link_next, link_copies = update(
        link_parts, link_state, link_gain, link_agg_weight, link_self_weight, link_out_weight, pairs
    )
    own = lax.all_to_all(link_copies, "col", 0, 0, tiled=True, axis_index_groups=same_core)
    other = lax.ppermute(own, "col", sibling)
    parts = flow_products(
        me, tile_flow, tile_link, tile_live, coefs, own, other, flow_blocks
    )
    flow_parts = sum_over_rows(*parts)
    (flow_next,) = update(
        flow_parts, flow_state, flow_gain, flow_agg_weight, flow_self_weight, flow_out_weight, 0
    )
    return (link_next, flow_next)


def gather_rows(state):
    sent = (state.astype(F32) * SCALE).astype(jnp.float16)
    got = lax.all_gather(sent, "row", axis=0, tiled=True)
    return (got.astype(F32) * (1 / SCALE)).astype(BF16)


def solution(mesh):
    return jax.shard_map(
        on_device,
        mesh=mesh,
        in_specs=(
            P(("col", "row"), None),
            P(("row", "col"), None),
            P("row", "col", None, None, None),
            P("row", "col", None),
            P("row", "col", None),
            P("row", "col", None),
            P(),
            P(),
            P(),
            P(),
            P(),
            P(),
            P(),
            P(),
        ),
        out_specs=(P(("row", "col"), None), P(("col", "row"), None)),
        check_vma=False,
    )
```

```python
import functools
import jax
import jax.numpy as jnp
from jax import lax
from jax.experimental import pallas as pl
from jax.experimental.pallas import tpu as pltpu
from jax.sharding import PartitionSpec as P

H = 256
BS = 128
VMEM = pl.BlockSpec(memory_space=pltpu.VMEM)
SMEM = pl.BlockSpec(memory_space=pltpu.SMEM)
PARAMS = pltpu.CompilerParams(vmem_limit_bytes=40 << 20)
F32 = jnp.float32
BF16 = jnp.bfloat16
SCALE = 8192.0


def link_products_kernel(
    me_ref, flow_ref, link_ref, live_ref, coefs_ref, pieces_ref, own_ref, other_ref, acc_ref
):
    blocks = acc_ref.shape[0] - 1
    half = blocks // 2
    acc_ref[...] = jnp.zeros_like(acc_ref)
    for slot in range(coefs_ref.shape[0]):
        block = link_ref[0, 0, slot]
        place = ((block + me_ref[1]) % 2) * half + block // 2
        place = jnp.where(live_ref[0, 0, slot] == 1, place, blocks)
        acc_ref[place] += lax.dot_general(
            coefs_ref[slot],
            pieces_ref[flow_ref[0, 0, slot]],
            (((0,), (0,)), ((), ())),
            preferred_element_type=F32,
        )
    own_ref[...] = acc_ref[:half].astype(BF16)
    other_ref[...] = acc_ref[half : 2 * half].astype(BF16)


def link_products(me, flow, link, live, coefs, pieces, blocks):
    shape = jax.ShapeDtypeStruct((blocks // 2, BS, H), BF16)
    return pl.pallas_call(
        link_products_kernel,
        out_shape=[shape, shape],
        in_specs=[SMEM, SMEM, SMEM, SMEM, VMEM, VMEM],
        out_specs=[VMEM, VMEM],
        scratch_shapes=[pltpu.VMEM((blocks + 1, BS, H), F32)],
        compiler_params=PARAMS,
        name="link_products",
    )(me, flow, link, live, coefs, pieces)


ROW_ORDER = (0, 5, -5, 2, 7, -3, -2, -7, 3, 1, 6, -4, -1, -6, 4, 8)


def flow_products_kernel(
    me_ref, flow_ref, link_ref, live_ref, coefs_ref, own_ref, other_ref, *rest
):
    *out_refs, acc_ref, pieces_ref, order_ref = rest
    blocks = acc_ref.shape[0] - 1
    rows = blocks // 2
    half = own_ref.shape[0]
    for place, ahead in enumerate(ROW_ORDER):
        order_ref[ahead % rows] = 2 * place
    pieces_ref[:half] = own_ref[...]
    pieces_ref[half:] = other_ref[...]
    acc_ref[...] = jnp.zeros_like(acc_ref)
    for slot in range(coefs_ref.shape[0]):
        block = flow_ref[0, 0, slot]
        ahead = jnp.where(me_ref[0] % 2 == 0, block // 2 - me_ref[0], me_ref[0] - block // 2)
        place = order_ref[(ahead + rows) % rows] + block % 2
        place = jnp.where(live_ref[0, 0, slot] == 1, place, blocks)
        piece = link_ref[0, 0, slot]
        piece = ((piece + me_ref[1]) % 2) * half + piece // 2
        acc_ref[place] += jnp.dot(
            coefs_ref[slot], pieces_ref[piece], preferred_element_type=F32
        )
    start = 0
    for out_ref in out_refs:
        count = out_ref.shape[0]
        out_ref[...] = acc_ref[start : start + count].astype(BF16)
        start += count


def flow_products(me, flow, link, live, coefs, own, other, blocks):
    assert blocks == 2 * len(ROW_ORDER)
    counts = [6] + [3] * 8 + [2]
    return pl.pallas_call(
        flow_products_kernel,
        out_shape=[jax.ShapeDtypeStruct((count, BS, H), BF16) for count in counts],
        in_specs=[SMEM, SMEM, SMEM, SMEM, VMEM, VMEM, VMEM],
        out_specs=[VMEM] * len(counts),
        scratch_shapes=[
            pltpu.VMEM((blocks + 1, BS, H), F32),
            pltpu.VMEM((2 * own.shape[0], BS, H), BF16),
            pltpu.SMEM((len(ROW_ORDER),), jnp.int32),
        ],
        compiler_params=PARAMS,
        name="flow_products",
    )(me, flow, link, live, coefs, own, other)


def add(*terms):
    total = terms[0].astype(F32)
    for term in terms[1:]:
        total = total + term.astype(F32)
    return total.astype(BF16)


def sum_over_rows(own, *parts):
    *two_a, two_b0, two_b1, one_a0, one_a1, one_b0, one_b1, opposite = parts
    rows = len(ROW_ORDER)

    def swap_a(x, step):
        pairs = [(i, (i + step if i % 2 == 0 else i - step) % rows) for i in range(rows)]
        return lax.ppermute(x, "row", pairs)

    def swap_b(x, step):
        pairs = [(i, (i - step if i % 2 == 0 else i + step) % rows) for i in range(rows)]
        return lax.ppermute(x, "row", pairs)

    two_a0, two_a1 = two_a
    got_a0, got_b0 = swap_a(two_a0, 1), swap_b(two_b0, 1)
    got_a1, got_b1 = swap_a(two_a1, 1), swap_b(two_b1, 1)
    opposite = swap_a(opposite, 3)
    one_b0, one_a0 = swap_b(add(one_b0, got_a0), 1), swap_a(add(one_a0, got_b0), 1)
    one_b1 = swap_b(add(one_b1, got_a1), 1)
    got_b1, opposite = lax.optimization_barrier((got_b1, opposite))
    one_a1 = swap_a(add(one_a1, got_b1), 1)
    got_a = jnp.concatenate([one_a0, one_a1], axis=0)
    got_b = jnp.concatenate([one_b0, one_b1], axis=0)
    mine = add(own[:2], got_a[:2], got_b[:2])
    far_a = add(own[2:4], got_a[4:6], got_b[2:4])
    far_b = add(own[4:6], got_a[2:4], got_b[4:6], opposite)
    got_a, got_b = swap_a(far_a, 5), swap_b(far_b, 5)
    return jnp.stack([x.reshape(2 * BS, H) for x in (mine, got_a, got_b)])


def add_kernel(a_ref, b_ref, out_ref):
    out_ref[...] = (a_ref[...].astype(F32) + b_ref[...].astype(F32)).astype(BF16)


def add_two(a, b):
    return pl.pallas_call(
        add_kernel,
        out_shape=jax.ShapeDtypeStruct(a.shape, BF16),
        in_specs=[VMEM, VMEM],
        out_specs=VMEM,
        compiler_params=PARAMS,
        name="add_two",
    )(a, b)


def update_kernel(parts_ref, state_ref, gain_ref, agg_ref, self_ref, out_w_ref, *out_refs):
    totals = jnp.sum(parts_ref[...].astype(F32), axis=0)
    scale = lax.rsqrt(jnp.mean(totals * totals, axis=-1, keepdims=True) + 1e-05)
    normed = (totals * scale * gain_ref[...]).astype(BF16)
    before = jnp.dot(normed, agg_ref[...], preferred_element_type=F32) + jnp.dot(
        state_ref[...], self_ref[...], preferred_element_type=F32
    )
    hidden = jax.nn.silu(before).astype(BF16)
    result = (
        state_ref[...].astype(F32)
        + jnp.dot(hidden, out_w_ref[...], preferred_element_type=F32)
    ).astype(BF16)
    out_refs[0][...] = result
    if len(out_refs) > 1:
        for copy in range(out_refs[1].shape[0]):
            out_refs[1][copy] = result


def update(parts, state, gain, agg_weight, self_weight, out_weight, copies):
    shapes = [jax.ShapeDtypeStruct(state.shape, BF16)]
    if copies:
        shapes.append(jax.ShapeDtypeStruct((copies,) + state.shape, BF16))
    return pl.pallas_call(
        update_kernel,
        out_shape=shapes,
        in_specs=[VMEM] * 6,
        out_specs=[VMEM] * len(shapes),
        compiler_params=PARAMS,
        name="link_update" if copies else "flow_update",
    )(parts, state, gain.reshape(1, H), agg_weight, self_weight, out_weight)


def on_device(
    flow_state,
    link_state,
    incidence,
    tile_flow,
    tile_link,
    tile_live,
    link_gain,
    link_agg_weight,
    link_self_weight,
    link_out_weight,
    flow_gain,
    flow_agg_weight,
    flow_self_weight,
    flow_out_weight,
):
    coefs = incidence[0, 0]
    cols = lax.axis_size("col")
    rows = lax.axis_size("row")
    pairs = cols // 2
    flow_blocks = flow_state.shape[0] // BS * rows
    me = jnp.stack([lax.axis_index("row"), lax.axis_index("col") % 2]).astype(jnp.int32)
    sibling = [(i, i ^ 1) for i in range(cols)]
    same_core = [[2 * i + core for i in range(pairs)] for core in range(2)]

    flow_group = gather_rows(flow_state)
    own, other = link_products(
        me, tile_flow, tile_link, tile_live, coefs,
        flow_group.reshape(flow_blocks, BS, H), cols,
    )
    own = add_two(own, lax.ppermute(other, "col", sibling))
    link_parts = lax.all_to_all(own, "col", 0, 0, tiled=True, axis_index_groups=same_core)
    link_next, link_copies = update(
        link_parts, link_state, link_gain, link_agg_weight, link_self_weight, link_out_weight, pairs
    )
    own = lax.all_to_all(link_copies, "col", 0, 0, tiled=True, axis_index_groups=same_core)
    other = lax.ppermute(own, "col", sibling)
    parts = flow_products(
        me, tile_flow, tile_link, tile_live, coefs, own, other, flow_blocks
    )
    flow_parts = sum_over_rows(*parts)
    (flow_next,) = update(
        flow_parts, flow_state, flow_gain, flow_agg_weight, flow_self_weight, flow_out_weight, 0
    )
    return (link_next, flow_next)


def gather_rows(state):
    sent = (state.astype(F32) * SCALE).astype(jnp.float16)
    got = lax.all_gather(sent, "row", axis=0, tiled=True)
    return (got.astype(F32) * (1 / SCALE)).astype(BF16)


def solution(mesh):
    return jax.shard_map(
        on_device,
        mesh=mesh,
        in_specs=(
            P(("col", "row"), None),
            P(("row", "col"), None),
            P("row", "col", None, None, None),
            P("row", "col", None),
            P("row", "col", None),
            P("row", "col", None),
            P(),
            P(),
            P(),
            P(),
            P(),
            P(),
            P(),
            P(),
        ),
        out_specs=(P(("row", "col"), None), P(("col", "row"), None)),
        check_vma=False,
    )
```

```python
import functools
import jax
import jax.numpy as jnp
from jax import lax
from jax.experimental import pallas as pl
from jax.experimental.pallas import tpu as pltpu
from jax.sharding import PartitionSpec as P

H = 256
BS = 128
VMEM = pl.BlockSpec(memory_space=pltpu.VMEM)
SMEM = pl.BlockSpec(memory_space=pltpu.SMEM)
PARAMS = pltpu.CompilerParams(vmem_limit_bytes=40 << 20)
F32 = jnp.float32
BF16 = jnp.bfloat16
SCALE = 8192.0


def link_products_kernel(
    me_ref, flow_ref, link_ref, live_ref, coefs_ref, pieces_ref, own_ref, other_ref, acc_ref
):
    blocks = acc_ref.shape[0] - 1
    half = blocks // 2
    acc_ref[...] = jnp.zeros_like(acc_ref)
    for slot in range(coefs_ref.shape[0]):
        block = link_ref[0, 0, slot]
        place = ((block + me_ref[1]) % 2) * half + block // 2
        place = jnp.where(live_ref[0, 0, slot] == 1, place, blocks)
        acc_ref[place] += lax.dot_general(
            coefs_ref[slot],
            pieces_ref[flow_ref[0, 0, slot]],
            (((0,), (0,)), ((), ())),
            preferred_element_type=F32,
        )
    own_ref[...] = acc_ref[:half].astype(BF16)
    other_ref[...] = acc_ref[half : 2 * half].astype(BF16)


def link_products(me, flow, link, live, coefs, pieces, blocks):
    shape = jax.ShapeDtypeStruct((blocks // 2, BS, H), BF16)
    return pl.pallas_call(
        link_products_kernel,
        out_shape=[shape, shape],
        in_specs=[SMEM, SMEM, SMEM, SMEM, VMEM, VMEM],
        out_specs=[VMEM, VMEM],
        scratch_shapes=[pltpu.VMEM((blocks + 1, BS, H), F32)],
        compiler_params=PARAMS,
        name="link_products",
    )(me, flow, link, live, coefs, pieces)


ROW_ORDER = (0, 3, 6, -3, -6, 1, 4, 7, -2, -5, -1, -4, -7, 2, 5, 8)


def flow_products_kernel(
    me_ref, flow_ref, link_ref, live_ref, coefs_ref, own_ref, other_ref, *rest
):
    *out_refs, acc_ref, pieces_ref, order_ref = rest
    blocks = acc_ref.shape[0] - 1
    rows = blocks // 2
    half = own_ref.shape[0]
    for place, ahead in enumerate(ROW_ORDER):
        order_ref[ahead % rows] = 2 * place
    pieces_ref[:half] = own_ref[...]
    pieces_ref[half:] = other_ref[...]
    acc_ref[...] = jnp.zeros_like(acc_ref)
    for slot in range(coefs_ref.shape[0]):
        block = flow_ref[0, 0, slot]
        ahead = jnp.where(me_ref[0] % 2 == 0, block // 2 - me_ref[0], me_ref[0] - block // 2)
        place = order_ref[(ahead + rows) % rows] + block % 2
        place = jnp.where(live_ref[0, 0, slot] == 1, place, blocks)
        piece = link_ref[0, 0, slot]
        piece = ((piece + me_ref[1]) % 2) * half + piece // 2
        acc_ref[place] += jnp.dot(
            coefs_ref[slot], pieces_ref[piece], preferred_element_type=F32
        )
    start = 0
    for out_ref in out_refs:
        count = out_ref.shape[0]
        out_ref[...] = acc_ref[start : start + count].astype(BF16)
        start += count


def flow_products(me, flow, link, live, coefs, own, other, blocks):
    assert blocks == 2 * len(ROW_ORDER)
    counts = [10, 10, 10, 2]
    return pl.pallas_call(
        flow_products_kernel,
        out_shape=[jax.ShapeDtypeStruct((count, BS, H), BF16) for count in counts],
        in_specs=[SMEM, SMEM, SMEM, SMEM, VMEM, VMEM, VMEM],
        out_specs=[VMEM] * len(counts),
        scratch_shapes=[
            pltpu.VMEM((blocks + 1, BS, H), F32),
            pltpu.VMEM((2 * own.shape[0], BS, H), BF16),
            pltpu.SMEM((len(ROW_ORDER),), jnp.int32),
        ],
        compiler_params=PARAMS,
        name="flow_products",
    )(me, flow, link, live, coefs, own, other)


def add(*terms):
    total = terms[0].astype(F32)
    for term in terms[1:]:
        total = total + term.astype(F32)
    return total.astype(BF16)


def sum_over_rows(own, for_a, for_b, opposite):
    rows = len(ROW_ORDER)

    def swap_a(x, step):
        pairs = [(i, (i + step if i % 2 == 0 else i - step) % rows) for i in range(rows)]
        return lax.ppermute(x, "row", pairs)

    def swap_b(x, step):
        pairs = [(i, (i - step if i % 2 == 0 else i + step) % rows) for i in range(rows)]
        return lax.ppermute(x, "row", pairs)

    got_a, got_b = swap_a(for_a, 1), swap_b(for_b, 1)
    opposite = swap_a(opposite, 2)
    six_a = add(own[4:6], got_a[8:10], got_b[4:6], opposite)
    six_b = add(own[8:10], got_a[4:6], got_b[8:10])
    mine = add(own[:2], got_a[:2], got_b[:2])
    three_a = own[2:4].astype(F32) + got_a[6:8].astype(F32) + got_b[2:4].astype(F32)
    three_b = own[6:8].astype(F32) + got_a[2:4].astype(F32) + got_b[6:8].astype(F32)
    got_a, got_b = swap_a(six_a, 3), swap_b(six_b, 3)
    three_b, three_a = add(three_b, got_a), add(three_a, got_b)
    got_a, got_b = swap_a(three_a, 3), swap_b(three_b, 3)
    return jnp.stack([x.reshape(2 * BS, H) for x in (mine, got_a, got_b)])


def add_kernel(a_ref, b_ref, out_ref):
    out_ref[...] = (a_ref[...].astype(F32) + b_ref[...].astype(F32)).astype(BF16)


def add_two(a, b):
    return pl.pallas_call(
        add_kernel,
        out_shape=jax.ShapeDtypeStruct(a.shape, BF16),
        in_specs=[VMEM, VMEM],
        out_specs=VMEM,
        compiler_params=PARAMS,
        name="add_two",
    )(a, b)


def update_kernel(parts_ref, state_ref, gain_ref, agg_ref, self_ref, out_w_ref, *out_refs):
    totals = jnp.sum(parts_ref[...].astype(F32), axis=0)
    scale = lax.rsqrt(jnp.mean(totals * totals, axis=-1, keepdims=True) + 1e-05)
    normed = (totals * scale * gain_ref[...]).astype(BF16)
    before = jnp.dot(normed, agg_ref[...], preferred_element_type=F32) + jnp.dot(
        state_ref[...], self_ref[...], preferred_element_type=F32
    )
    hidden = jax.nn.silu(before).astype(BF16)
    result = (
        state_ref[...].astype(F32)
        + jnp.dot(hidden, out_w_ref[...], preferred_element_type=F32)
    ).astype(BF16)
    out_refs[0][...] = result
    if len(out_refs) > 1:
        for copy in range(out_refs[1].shape[0]):
            out_refs[1][copy] = result


def update(parts, state, gain, agg_weight, self_weight, out_weight, copies):
    shapes = [jax.ShapeDtypeStruct(state.shape, BF16)]
    if copies:
        shapes.append(jax.ShapeDtypeStruct((copies,) + state.shape, BF16))
    return pl.pallas_call(
        update_kernel,
        out_shape=shapes,
        in_specs=[VMEM] * 6,
        out_specs=[VMEM] * len(shapes),
        compiler_params=PARAMS,
        name="link_update" if copies else "flow_update",
    )(parts, state, gain.reshape(1, H), agg_weight, self_weight, out_weight)


def on_device(
    flow_state,
    link_state,
    incidence,
    tile_flow,
    tile_link,
    tile_live,
    link_gain,
    link_agg_weight,
    link_self_weight,
    link_out_weight,
    flow_gain,
    flow_agg_weight,
    flow_self_weight,
    flow_out_weight,
):
    coefs = incidence[0, 0]
    cols = lax.axis_size("col")
    rows = lax.axis_size("row")
    pairs = cols // 2
    flow_blocks = flow_state.shape[0] // BS * rows
    me = jnp.stack([lax.axis_index("row"), lax.axis_index("col") % 2]).astype(jnp.int32)
    sibling = [(i, i ^ 1) for i in range(cols)]
    same_core = [[2 * i + core for i in range(pairs)] for core in range(2)]

    flow_group = gather_rows(flow_state)
    own, other = link_products(
        me, tile_flow, tile_link, tile_live, coefs,
        flow_group.reshape(flow_blocks, BS, H), cols,
    )
    own = add_two(own, lax.ppermute(other, "col", sibling))
    link_parts = lax.all_to_all(own, "col", 0, 0, tiled=True, axis_index_groups=same_core)
    link_next, link_copies = update(
        link_parts, link_state, link_gain, link_agg_weight, link_self_weight, link_out_weight, pairs
    )
    own = lax.all_to_all(link_copies, "col", 0, 0, tiled=True, axis_index_groups=same_core)
    other = lax.ppermute(own, "col", sibling)
    parts = flow_products(
        me, tile_flow, tile_link, tile_live, coefs, own, other, flow_blocks
    )
    flow_parts = sum_over_rows(*parts)
    (flow_next,) = update(
        flow_parts, flow_state, flow_gain, flow_agg_weight, flow_self_weight, flow_out_weight, 0
    )
    return (link_next, flow_next)


def gather_rows(state):
    sent = (state.astype(F32) * SCALE).astype(jnp.float16)
    got = lax.all_gather(sent, "row", axis=0, tiled=True)
    return (got.astype(F32) * (1 / SCALE)).astype(BF16)


def solution(mesh):
    return jax.shard_map(
        on_device,
        mesh=mesh,
        in_specs=(
            P(("col", "row"), None),
            P(("row", "col"), None),
            P("row", "col", None, None, None),
            P("row", "col", None),
            P("row", "col", None),
            P("row", "col", None),
            P(),
            P(),
            P(),
            P(),
            P(),
            P(),
            P(),
            P(),
        ),
        out_specs=(P(("row", "col"), None), P(("col", "row"), None)),
        check_vma=False,
    )
```

```python
import functools
import jax
import jax.numpy as jnp
from jax import lax
from jax.experimental import pallas as pl
from jax.experimental.pallas import tpu as pltpu
from jax.sharding import PartitionSpec as P

H = 256
BS = 128
VMEM = pl.BlockSpec(memory_space=pltpu.VMEM)
SMEM = pl.BlockSpec(memory_space=pltpu.SMEM)
PARAMS = pltpu.CompilerParams(vmem_limit_bytes=40 << 20)
F32 = jnp.float32
BF16 = jnp.bfloat16
SCALE = 8192.0


def link_products_kernel(
    me_ref, flow_ref, link_ref, live_ref, coefs_ref, pieces_ref, own_ref, other_ref, acc_ref
):
    blocks = acc_ref.shape[0] - 1
    half = blocks // 2
    acc_ref[...] = jnp.zeros_like(acc_ref)
    for slot in range(coefs_ref.shape[0]):
        block = link_ref[0, 0, slot]
        place = ((block + me_ref[1]) % 2) * half + block // 2
        place = jnp.where(live_ref[0, 0, slot] == 1, place, blocks)
        acc_ref[place] += lax.dot_general(
            coefs_ref[slot],
            pieces_ref[flow_ref[0, 0, slot]],
            (((0,), (0,)), ((), ())),
            preferred_element_type=F32,
        )
    own_ref[...] = acc_ref[:half].astype(BF16)
    other_ref[...] = acc_ref[half : 2 * half].astype(BF16)


def link_products(me, flow, link, live, coefs, pieces, blocks):
    shape = jax.ShapeDtypeStruct((blocks // 2, BS, H), BF16)
    return pl.pallas_call(
        link_products_kernel,
        out_shape=[shape, shape],
        in_specs=[SMEM, SMEM, SMEM, SMEM, VMEM, VMEM],
        out_specs=[VMEM, VMEM],
        scratch_shapes=[pltpu.VMEM((blocks + 1, BS, H), F32)],
        compiler_params=PARAMS,
        name="link_products",
    )(me, flow, link, live, coefs, pieces)


ROW_ORDER = (0, 3, 6, -3, -6, 7, -5, 1, 4, -2, -7, 5, -1, -4, 2, 8)


def flow_products_kernel(
    me_ref, flow_ref, link_ref, live_ref, coefs_ref, own_ref, other_ref, *rest
):
    *out_refs, acc_ref, pieces_ref, order_ref = rest
    blocks = acc_ref.shape[0] - 1
    rows = blocks // 2
    half = own_ref.shape[0]
    for place, ahead in enumerate(ROW_ORDER):
        order_ref[ahead % rows] = 2 * place
    pieces_ref[:half] = own_ref[...]
    pieces_ref[half:] = other_ref[...]
    acc_ref[...] = jnp.zeros_like(acc_ref)
    for slot in range(coefs_ref.shape[0]):
        block = flow_ref[0, 0, slot]
        ahead = jnp.where(me_ref[0] % 2 == 0, block // 2 - me_ref[0], me_ref[0] - block // 2)
        place = order_ref[(ahead + rows) % rows] + block % 2
        place = jnp.where(live_ref[0, 0, slot] == 1, place, blocks)
        piece = link_ref[0, 0, slot]
        piece = ((piece + me_ref[1]) % 2) * half + piece // 2
        acc_ref[place] += jnp.dot(
            coefs_ref[slot], pieces_ref[piece], preferred_element_type=F32
        )
    start = 0
    for out_ref in out_refs:
        count = out_ref.shape[0]
        out_ref[...] = acc_ref[start : start + count].astype(BF16)
        start += count


def flow_products(me, flow, link, live, coefs, own, other, blocks):
    assert blocks == 2 * len(ROW_ORDER)
    counts = [10, 4, 6, 4, 6, 2]
    return pl.pallas_call(
        flow_products_kernel,
        out_shape=[jax.ShapeDtypeStruct((count, BS, H), BF16) for count in counts],
        in_specs=[SMEM, SMEM, SMEM, SMEM, VMEM, VMEM, VMEM],
        out_specs=[VMEM] * len(counts),
        scratch_shapes=[
            pltpu.VMEM((blocks + 1, BS, H), F32),
            pltpu.VMEM((2 * own.shape[0], BS, H), BF16),
            pltpu.SMEM((len(ROW_ORDER),), jnp.int32),
        ],
        compiler_params=PARAMS,
        name="flow_products",
    )(me, flow, link, live, coefs, own, other)


def add(*terms):
    total = terms[0].astype(F32)
    for term in terms[1:]:
        total = total + term.astype(F32)
    return total.astype(BF16)


def sum_over_rows(own, far_a, near_a, far_b, near_b, opposite):
    rows = len(ROW_ORDER)

    def swap_a(x, step):
        pairs = [(i, (i + step if i % 2 == 0 else i - step) % rows) for i in range(rows)]
        return lax.ppermute(x, "row", pairs)

    def swap_b(x, step):
        pairs = [(i, (i - step if i % 2 == 0 else i + step) % rows) for i in range(rows)]
        return lax.ppermute(x, "row", pairs)

    far_a, far_b = swap_a(far_a, 1), swap_b(far_b, 1)
    opposite = swap_a(opposite, 2)
    near_a, near_b = swap_a(near_a, 1), swap_b(near_b, 1)
    six_a = add(own[4:6], far_a[2:4], far_b[:2], opposite)
    six_b = add(own[8:10], far_a[:2], far_b[2:4])
    mine = add(own[:2], near_a[:2], near_b[:2])
    three_a = own[2:4].astype(F32) + near_a[4:6].astype(F32) + near_b[2:4].astype(F32)
    three_b = own[6:8].astype(F32) + near_a[2:4].astype(F32) + near_b[4:6].astype(F32)
    got_a, got_b = swap_a(six_a, 3), swap_b(six_b, 3)
    three_b, three_a = add(three_b, got_a), add(three_a, got_b)
    got_a, got_b = swap_a(three_a, 3), swap_b(three_b, 3)
    return jnp.stack([x.reshape(2 * BS, H) for x in (mine, got_a, got_b)])


def add_kernel(a_ref, b_ref, out_ref):
    out_ref[...] = (a_ref[...].astype(F32) + b_ref[...].astype(F32)).astype(BF16)


def add_two(a, b):
    return pl.pallas_call(
        add_kernel,
        out_shape=jax.ShapeDtypeStruct(a.shape, BF16),
        in_specs=[VMEM, VMEM],
        out_specs=VMEM,
        compiler_params=PARAMS,
        name="add_two",
    )(a, b)


def update_kernel(parts_ref, state_ref, gain_ref, agg_ref, self_ref, out_w_ref, *out_refs):
    totals = jnp.sum(parts_ref[...].astype(F32), axis=0)
    scale = lax.rsqrt(jnp.mean(totals * totals, axis=-1, keepdims=True) + 1e-05)
    normed = (totals * scale * gain_ref[...]).astype(BF16)
    before = jnp.dot(normed, agg_ref[...], preferred_element_type=F32) + jnp.dot(
        state_ref[...], self_ref[...], preferred_element_type=F32
    )
    hidden = jax.nn.silu(before).astype(BF16)
    result = (
        state_ref[...].astype(F32)
        + jnp.dot(hidden, out_w_ref[...], preferred_element_type=F32)
    ).astype(BF16)
    out_refs[0][...] = result
    if len(out_refs) > 1:
        for copy in range(out_refs[1].shape[0]):
            out_refs[1][copy] = result


def update(parts, state, gain, agg_weight, self_weight, out_weight, copies):
    shapes = [jax.ShapeDtypeStruct(state.shape, BF16)]
    if copies:
        shapes.append(jax.ShapeDtypeStruct((copies,) + state.shape, BF16))
    return pl.pallas_call(
        update_kernel,
        out_shape=shapes,
        in_specs=[VMEM] * 6,
        out_specs=[VMEM] * len(shapes),
        compiler_params=PARAMS,
        name="link_update" if copies else "flow_update",
    )(parts, state, gain.reshape(1, H), agg_weight, self_weight, out_weight)


def on_device(
    flow_state,
    link_state,
    incidence,
    tile_flow,
    tile_link,
    tile_live,
    link_gain,
    link_agg_weight,
    link_self_weight,
    link_out_weight,
    flow_gain,
    flow_agg_weight,
    flow_self_weight,
    flow_out_weight,
):
    coefs = incidence[0, 0]
    cols = lax.axis_size("col")
    rows = lax.axis_size("row")
    pairs = cols // 2
    flow_blocks = flow_state.shape[0] // BS * rows
    me = jnp.stack([lax.axis_index("row"), lax.axis_index("col") % 2]).astype(jnp.int32)
    sibling = [(i, i ^ 1) for i in range(cols)]
    same_core = [[2 * i + core for i in range(pairs)] for core in range(2)]

    flow_group = gather_rows(flow_state)
    own, other = link_products(
        me, tile_flow, tile_link, tile_live, coefs,
        flow_group.reshape(flow_blocks, BS, H), cols,
    )
    own = add_two(own, lax.ppermute(other, "col", sibling))
    link_parts = lax.all_to_all(own, "col", 0, 0, tiled=True, axis_index_groups=same_core)
    link_next, link_copies = update(
        link_parts, link_state, link_gain, link_agg_weight, link_self_weight, link_out_weight, pairs
    )
    own = lax.all_to_all(link_copies, "col", 0, 0, tiled=True, axis_index_groups=same_core)
    other = lax.ppermute(own, "col", sibling)
    parts = flow_products(
        me, tile_flow, tile_link, tile_live, coefs, own, other, flow_blocks
    )
    flow_parts = sum_over_rows(*parts)
    (flow_next,) = update(
        flow_parts, flow_state, flow_gain, flow_agg_weight, flow_self_weight, flow_out_weight, 0
    )
    return (link_next, flow_next)


def gather_rows(state):
    sent = (state.astype(F32) * SCALE).astype(jnp.float16)
    got = lax.all_gather(sent, "row", axis=0, tiled=True)
    return (got.astype(F32) * (1 / SCALE)).astype(BF16)


def solution(mesh):
    return jax.shard_map(
        on_device,
        mesh=mesh,
        in_specs=(
            P(("col", "row"), None),
            P(("row", "col"), None),
            P("row", "col", None, None, None),
            P("row", "col", None),
            P("row", "col", None),
            P("row", "col", None),
            P(),
            P(),
            P(),
            P(),
            P(),
            P(),
            P(),
            P(),
        ),
        out_specs=(P(("row", "col"), None), P(("col", "row"), None)),
        check_vma=False,
    )
```

```python
import functools
import jax
import jax.numpy as jnp
from jax import lax
from jax.experimental import pallas as pl
from jax.experimental.pallas import tpu as pltpu
from jax.sharding import PartitionSpec as P

H = 256
BS = 128
VMEM = pl.BlockSpec(memory_space=pltpu.VMEM)
SMEM = pl.BlockSpec(memory_space=pltpu.SMEM)
PARAMS = pltpu.CompilerParams(vmem_limit_bytes=40 << 20)
F32 = jnp.float32
BF16 = jnp.bfloat16
SCALE = 8192.0


def link_products_kernel(
    side, me_ref, flow_ref, link_ref, live_ref, coefs_ref, pieces_ref, out_ref, acc_ref
):
    half = acc_ref.shape[0] - 1
    acc_ref[...] = jnp.zeros_like(acc_ref)
    for slot in range(coefs_ref.shape[0]):
        block = link_ref[0, 0, slot]
        here = jnp.logical_and(live_ref[0, 0, slot] == 1, (block + me_ref[1]) % 2 == side)
        place = jnp.where(here, block // 2, half)
        acc_ref[place] += lax.dot_general(
            coefs_ref[slot],
            pieces_ref[flow_ref[0, 0, slot]],
            (((0,), (0,)), ((), ())),
            preferred_element_type=F32,
        )
    out_ref[...] = acc_ref[:half].astype(BF16)


def link_products(side, me, flow, link, live, coefs, pieces, blocks):
    shape = jax.ShapeDtypeStruct((blocks // 2, BS, H), BF16)
    return pl.pallas_call(
        functools.partial(link_products_kernel, side),
        out_shape=shape,
        in_specs=[SMEM, SMEM, SMEM, SMEM, VMEM, VMEM],
        out_specs=VMEM,
        scratch_shapes=[pltpu.VMEM((blocks // 2 + 1, BS, H), F32)],
        compiler_params=PARAMS,
        name="link_products",
    )(me, flow, link, live, coefs, pieces)


ROW_ORDER = (0, 3, 6, -3, -6, 7, -5, 1, 4, -2, -7, 5, -1, -4, 2, 8)


def flow_products_kernel(
    me_ref, flow_ref, link_ref, live_ref, coefs_ref, own_ref, other_ref, *rest
):
    *out_refs, acc_ref, pieces_ref, order_ref = rest
    blocks = acc_ref.shape[0] - 1
    rows = blocks // 2
    half = own_ref.shape[0]
    for place, ahead in enumerate(ROW_ORDER):
        order_ref[ahead % rows] = 2 * place
    pieces_ref[:half] = own_ref[...]
    pieces_ref[half:] = other_ref[...]
    acc_ref[...] = jnp.zeros_like(acc_ref)
    for slot in range(coefs_ref.shape[0]):
        block = flow_ref[0, 0, slot]
        ahead = jnp.where(me_ref[0] % 2 == 0, block // 2 - me_ref[0], me_ref[0] - block // 2)
        place = order_ref[(ahead + rows) % rows] + block % 2
        place = jnp.where(live_ref[0, 0, slot] == 1, place, blocks)
        piece = link_ref[0, 0, slot]
        piece = ((piece + me_ref[1]) % 2) * half + piece // 2
        acc_ref[place] += jnp.dot(
            coefs_ref[slot], pieces_ref[piece], preferred_element_type=F32
        )
    start = 0
    for out_ref in out_refs:
        count = out_ref.shape[0]
        out_ref[...] = acc_ref[start : start + count].astype(BF16)
        start += count


def flow_products(me, flow, link, live, coefs, own, other, blocks):
    assert blocks == 2 * len(ROW_ORDER)
    counts = [10, 4, 6, 4, 6, 2]
    return pl.pallas_call(
        flow_products_kernel,
        out_shape=[jax.ShapeDtypeStruct((count, BS, H), BF16) for count in counts],
        in_specs=[SMEM, SMEM, SMEM, SMEM, VMEM, VMEM, VMEM],
        out_specs=[VMEM] * len(counts),
        scratch_shapes=[
            pltpu.VMEM((blocks + 1, BS, H), F32),
            pltpu.VMEM((2 * own.shape[0], BS, H), BF16),
            pltpu.SMEM((len(ROW_ORDER),), jnp.int32),
        ],
        compiler_params=PARAMS,
        name="flow_products",
    )(me, flow, link, live, coefs, own, other)


def add(*terms):
    total = terms[0].astype(F32)
    for term in terms[1:]:
        total = total + term.astype(F32)
    return total.astype(BF16)


def sum_over_rows(own, far_a, near_a, far_b, near_b, opposite):
    rows = len(ROW_ORDER)

    def swap_a(x, step):
        pairs = [(i, (i + step if i % 2 == 0 else i - step) % rows) for i in range(rows)]
        return lax.ppermute(x, "row", pairs)

    def swap_b(x, step):
        pairs = [(i, (i - step if i % 2 == 0 else i + step) % rows) for i in range(rows)]
        return lax.ppermute(x, "row", pairs)

    far_a, far_b = swap_a(far_a, 1), swap_b(far_b, 1)
    opposite = swap_a(opposite, 2)
    near_a, near_b = swap_a(near_a, 1), swap_b(near_b, 1)
    six_a = add(own[4:6], far_a[2:4], far_b[:2], opposite)
    six_b = add(own[8:10], far_a[:2], far_b[2:4])
    mine = add(own[:2], near_a[:2], near_b[:2])
    three_a = own[2:4].astype(F32) + near_a[4:6].astype(F32) + near_b[2:4].astype(F32)
    three_b = own[6:8].astype(F32) + near_a[2:4].astype(F32) + near_b[4:6].astype(F32)
    got_a, got_b = swap_a(six_a, 3), swap_b(six_b, 3)
    three_b, three_a = add(three_b, got_a), add(three_a, got_b)
    got_a, got_b = swap_a(three_a, 3), swap_b(three_b, 3)
    return jnp.stack([x.reshape(2 * BS, H) for x in (mine, got_a, got_b)])


def add_kernel(a_ref, b_ref, out_ref):
    out_ref[...] = (a_ref[...].astype(F32) + b_ref[...].astype(F32)).astype(BF16)


def add_two(a, b):
    return pl.pallas_call(
        add_kernel,
        out_shape=jax.ShapeDtypeStruct(a.shape, BF16),
        in_specs=[VMEM, VMEM],
        out_specs=VMEM,
        compiler_params=PARAMS,
        name="add_two",
    )(a, b)


def update_kernel(parts_ref, state_ref, gain_ref, agg_ref, self_ref, out_w_ref, *out_refs):
    totals = jnp.sum(parts_ref[...].astype(F32), axis=0)
    scale = lax.rsqrt(jnp.mean(totals * totals, axis=-1, keepdims=True) + 1e-05)
    normed = (totals * scale * gain_ref[...]).astype(BF16)
    before = jnp.dot(normed, agg_ref[...], preferred_element_type=F32) + jnp.dot(
        state_ref[...], self_ref[...], preferred_element_type=F32
    )
    hidden = jax.nn.silu(before).astype(BF16)
    result = (
        state_ref[...].astype(F32)
        + jnp.dot(hidden, out_w_ref[...], preferred_element_type=F32)
    ).astype(BF16)
    out_refs[0][...] = result
    if len(out_refs) > 1:
        for copy in range(out_refs[1].shape[0]):
            out_refs[1][copy] = result


def update(parts, state, gain, agg_weight, self_weight, out_weight, copies):
    shapes = [jax.ShapeDtypeStruct(state.shape, BF16)]
    if copies:
        shapes.append(jax.ShapeDtypeStruct((copies,) + state.shape, BF16))
    return pl.pallas_call(
        update_kernel,
        out_shape=shapes,
        in_specs=[VMEM] * 6,
        out_specs=[VMEM] * len(shapes),
        compiler_params=PARAMS,
        name="link_update" if copies else "flow_update",
    )(parts, state, gain.reshape(1, H), agg_weight, self_weight, out_weight)


def on_device(
    flow_state,
    link_state,
    incidence,
    tile_flow,
    tile_link,
    tile_live,
    link_gain,
    link_agg_weight,
    link_self_weight,
    link_out_weight,
    flow_gain,
    flow_agg_weight,
    flow_self_weight,
    flow_out_weight,
):
    coefs = incidence[0, 0]
    cols = lax.axis_size("col")
    rows = lax.axis_size("row")
    pairs = cols // 2
    flow_blocks = flow_state.shape[0] // BS * rows
    me = jnp.stack([lax.axis_index("row"), lax.axis_index("col") % 2]).astype(jnp.int32)
    sibling = [(i, i ^ 1) for i in range(cols)]
    same_core = [[2 * i + core for i in range(pairs)] for core in range(2)]

    flow_group = gather_rows(flow_state)
    other, own = (
        link_products(
            side, me, tile_flow, tile_link, tile_live, coefs,
            flow_group.reshape(flow_blocks, BS, H), cols,
        )
        for side in (1, 0)
    )
    own = add_two(own, lax.ppermute(other, "col", sibling))
    link_parts = lax.all_to_all(own, "col", 0, 0, tiled=True, axis_index_groups=same_core)
    link_next, link_copies = update(
        link_parts, link_state, link_gain, link_agg_weight, link_self_weight, link_out_weight, pairs
    )
    own = lax.all_to_all(link_copies, "col", 0, 0, tiled=True, axis_index_groups=same_core)
    other = lax.ppermute(own, "col", sibling)
    parts = flow_products(
        me, tile_flow, tile_link, tile_live, coefs, own, other, flow_blocks
    )
    flow_parts = sum_over_rows(*parts)
    (flow_next,) = update(
        flow_parts, flow_state, flow_gain, flow_agg_weight, flow_self_weight, flow_out_weight, 0
    )
    return (link_next, flow_next)


def gather_rows(state):
    sent = (state.astype(F32) * SCALE).astype(jnp.float16)
    got = lax.all_gather(sent, "row", axis=0, tiled=True)
    return (got.astype(F32) * (1 / SCALE)).astype(BF16)


def solution(mesh):
    return jax.shard_map(
        on_device,
        mesh=mesh,
        in_specs=(
            P(("col", "row"), None),
            P(("row", "col"), None),
            P("row", "col", None, None, None),
            P("row", "col", None),
            P("row", "col", None),
            P("row", "col", None),
            P(),
            P(),
            P(),
            P(),
            P(),
            P(),
            P(),
            P(),
        ),
        out_specs=(P(("row", "col"), None), P(("col", "row"), None)),
        check_vma=False,
    )
```
